32 devices in a mesh: group: 4 (over x, core), block: 8 (over z, y).
Axes of the slice: x: 2, y: 2, z: 4, core: 2. Of those that a mesh axis runs over, the one named last changes fastest.
Arguments:
- flow_state: float32 [32, 7, 8, 8, 128], P(('group', 'block')), may hold values from -0.8 to 8, as said below
- adjoint: float32 [32, 7, 8, 8, 128], P(('group', 'block')), may hold values from -1.8 to 1.8
- cell_codes: int32 [32, 8, 8, 128], P(('group', 'block')), may hold values from 0 to 2, as said below
- block_links: int32 [32, 4, 2], P(('group', 'block')), may hold values from -1 to 31, as said below
- farfield: float32 [7], replicated, may hold values from -0.05 to 2, as said below
Outputs:
- gradient: float32 [32, 7, 8, 8, 128], P(('group', 'block'))
The draws below stay inside these ranges and needn't reach their ends.
Inputs may be any that keep to these rules, and one draw needn't show every extreme that they name: `flow_state`: components 0 to 6 are density (0.7 to 1.4), three velocities (-0.8 to 2), pressure (0.6 to 1.6), kt (0.005 to 0.2) and om (0.3 to 8). `farfield`: density 0.9 to 1.1, velocities -0.05 to 0.3, pressure 0.9 to 1.1, kt 0.005 to 0.02, om 0.5 to 2. `cell_codes`: codes are 0, 1 or 2. Block b lies in group b // 8. Where p = block_links[b, f, 0] >= 0, block p's face (f xor 1) names b with the same orientation; faces 0 and 1 name blocks of the previous and the next group, faces 2 and 3 blocks of b's own group; -1 marks a boundary face (face 0 of the first group, face 1 of the last, and the two ends of each group's radial chain). Column 1 is 0 or 1, and 0 where column 0 is -1.
All inputs are finite; a program needn't handle non-finite values.
Results may differ from the reference program's by a relative error of at most 0.0003.
Values sent between devices are 32-bit elements; how exact they have to be, the bound alone decides.
No kernel may reach another device: no remote copies, remote signals or barrier semaphores. Data moves between devices by JAX's collectives and lax.ppermute only.
A program may use at most 64 MiB of HBM per device.

```python
import math
import jax
import jax.numpy as jnp
from jax import lax

SIDE = 8
AZ = 128
NV = 7
GROUPS = 4
PER_GROUP = 8
BLOCKS = 32


def draw_flow_state(key, part):
    pieces = jax.random.split(key, 7)
    grid_shape = (BLOCKS, SIDE, SIDE, AZ)
    density = jax.random.uniform(pieces[0], grid_shape, jnp.float32, 0.8, 1.25)
    axial_speed = jnp.clip(0.8 + 0.3 * jax.random.normal(pieces[1], grid_shape, jnp.float32), -0.5, 2.0)
    radial_speed = jnp.clip(0.25 * jax.random.normal(pieces[2], grid_shape, jnp.float32), -0.8, 0.8)
    swirl_speed = jnp.clip(0.25 * jax.random.normal(pieces[3], grid_shape, jnp.float32), -0.8, 0.8)
    pressure = jax.random.uniform(pieces[4], grid_shape, jnp.float32, 0.7, 1.4)
    kinetic = jnp.exp(jax.random.uniform(pieces[5], grid_shape, jnp.float32, math.log(0.01), math.log(0.1)))
    omega = jnp.exp(jax.random.uniform(pieces[6], grid_shape, jnp.float32, math.log(0.5), math.log(5.0)))
    return jnp.stack([density, axial_speed, radial_speed, swirl_speed, pressure, kinetic, omega], axis=1)


def draw_cell_codes(key, part):
    rolled = jax.random.randint(key, (BLOCKS, SIDE, SIDE, AZ), 0, 16)
    return jnp.where(rolled == 0, 1, jnp.where(rolled < 4, 2, 0)).astype(jnp.int32)


def draw_farfield(key, part):
    pieces = jax.random.split(key, 7)
    lows = [0.9, 0.1, -0.05, -0.05, 0.9, 0.005, 0.5]
    highs = [1.1, 0.3, 0.05, 0.05, 1.1, 0.02, 2.0]
    values = [jax.random.uniform(pieces[member], (), jnp.float32, lows[member], highs[member]) for member in range(7)]
    return jnp.stack(values)


def draw_block_links(key, part):
    pieces = jax.random.split(key, 4)
    axial_perm = jax.vmap(lambda group_key: jax.random.permutation(group_key, PER_GROUP))(jax.random.split(pieces[0], GROUPS)).astype(jnp.int32)
    chain_order = jax.vmap(lambda group_key: jax.random.permutation(group_key, PER_GROUP))(jax.random.split(pieces[1], GROUPS)).astype(jnp.int32)
    axial_turn = jax.random.randint(pieces[2], (GROUPS, PER_GROUP), 0, 2).astype(jnp.int32)
    chain_turn = jax.random.randint(pieces[3], (GROUPS, PER_GROUP), 0, 2).astype(jnp.int32)
    axial_back = jnp.argsort(axial_perm, axis=1).astype(jnp.int32)
    position = jnp.argsort(chain_order, axis=1).astype(jnp.int32)
    group_ids = jnp.arange(GROUPS, dtype=jnp.int32)[:, None]
    zero_row = jnp.zeros((1, PER_GROUP), jnp.int32)
    back_prev = jnp.concatenate([zero_row, axial_back[:-1]], axis=0)
    turn_prev = jnp.concatenate([zero_row, axial_turn[:-1]], axis=0)
    has_prev = group_ids > 0
    has_next = group_ids < GROUPS - 1
    before_axial = jnp.where(has_prev, (group_ids - 1) * PER_GROUP + back_prev, -1)
    before_axial_turn = jnp.where(has_prev, jnp.take_along_axis(turn_prev, back_prev, axis=1), 0)
    after_axial = jnp.where(has_next, (group_ids + 1) * PER_GROUP + axial_perm, -1)
    after_axial_turn = jnp.where(has_next, axial_turn, 0)
    up_position = jnp.minimum(position + 1, PER_GROUP - 1)
    down_position = jnp.maximum(position - 1, 0)
    has_up = position < PER_GROUP - 1
    has_down = position > 0
    after_radial = jnp.where(has_up, group_ids * PER_GROUP + jnp.take_along_axis(chain_order, up_position, axis=1), -1)
    after_radial_turn = jnp.where(has_up, jnp.take_along_axis(chain_turn, position, axis=1), 0)
    before_radial = jnp.where(has_down, group_ids * PER_GROUP + jnp.take_along_axis(chain_order, down_position, axis=1), -1)
    before_radial_turn = jnp.where(has_down, jnp.take_along_axis(chain_turn, down_position, axis=1), 0)
    partners = jnp.stack([before_axial, after_axial, before_radial, after_radial], axis=-1).reshape(BLOCKS, 4)
    turnings = jnp.stack([before_axial_turn, after_axial_turn, before_radial_turn, after_radial_turn], axis=-1).reshape(BLOCKS, 4)
    return jnp.stack([partners, turnings], axis=-1).astype(jnp.int32)


def steps_of(stream_key, dims, cuts, smallest, top_value):
    factor_of = 1.0
    for axis_at, blocks in cuts:
        steps = jax.random.uniform(jax.random.fold_in(jax.random.fold_in(stream_key, 6), axis_at), (blocks,), jnp.float32, smallest / len(cuts), top_value / len(cuts))
        factor_of = factor_of * jnp.repeat(jnp.exp(steps), dims[axis_at] // blocks).reshape((-1,) + (1,) * (len(dims) - 1 - axis_at))
    return factor_of


def centred(key, dims, scale, limit, shards=(), kind=jnp.bfloat16):
    values = scale * jax.random.normal(key, dims, jnp.float32)
    if shards:
        values = values * steps_of(key, dims, shards, -0.22, 0.18)
    return jnp.clip(values, -limit, limit).astype(kind)


def setup_inputs(seed: int = 0) -> dict:
    splits = jax.random.split(jax.random.key(seed), 6)
    flow_state = draw_flow_state(jax.random.fold_in(splits[5], 71), 0)
    adjoint = centred(splits[1], (BLOCKS, NV, SIDE, SIDE, AZ), 0.3, 1.8, ((0, 32),), jnp.float32)
    cell_codes = draw_cell_codes(jax.random.fold_in(splits[5], 71), 0)
    block_links = draw_block_links(jax.random.fold_in(splits[5], 71), 0)
    farfield = draw_farfield(jax.random.fold_in(splits[5], 71), 0)
    return dict(flow_state=flow_state, adjoint=adjoint, cell_codes=cell_codes, block_links=block_links, farfield=farfield)


GAMMA = 1.4
MU_LAMINAR = 0.02
KAPPA_HEAT = 0.07
SIGMA_K = 0.85
SIGMA_OMEGA = 0.5
BETA_STAR = 0.09
BETA_OMEGA = 0.075
ALPHA_OMEGA = 0.52
LIMIT_A1 = 0.31
DAMPING = 2.0

def conserved(values):
    density = values[0]
    speed_sq = values[1] * values[1] + values[2] * values[2] + values[3] * values[3]
    energy = values[4] / (GAMMA - 1.0) + 0.5 * density * speed_sq
    return jnp.stack([density, density * values[1], density * values[2], density * values[3], energy, density * values[5], density * values[6]])

def normal_flux(values, normal_axis, normal_side):
    state_sum = conserved(values)
    normal_speed = normal_side * values[1 + normal_axis]
    columns = [state_sum[member] * normal_speed for member in range(7)]
    columns[1 + normal_axis] = columns[1 + normal_axis] + normal_side * values[4]
    columns[4] = columns[4] + values[4] * normal_speed
    return (jnp.stack(columns), state_sum, normal_speed)

def pair_term(centre, opposite, normal_axis, normal_side):
    flux_centre, cons_centre, speed_centre = normal_flux(centre, normal_axis, normal_side)
    flux_opposite, cons_opposite, speed_opposite = normal_flux(opposite, normal_axis, normal_side)
    sound_centre = jnp.sqrt(GAMMA * centre[4] / centre[0])
    sound_opposite = jnp.sqrt(GAMMA * opposite[4] / opposite[0])
    spread = 0.5 * (jnp.abs(speed_centre) + jnp.abs(speed_opposite) + sound_centre + sound_opposite)
    convect = 0.5 * (flux_centre + flux_opposite) - 0.5 * spread * (cons_opposite - cons_centre)
    velocity_jump = opposite[1:4] - centre[1:4]
    strain = lax.optimization_barrier(jnp.sum(velocity_jump * velocity_jump, axis=0))
    density_mean = 0.5 * (centre[0] + opposite[0])
    kinetic_mean = 0.5 * (centre[5] + opposite[5])
    omega_mean = 0.5 * (centre[6] + opposite[6])
    eddy_visc = density_mean * kinetic_mean / jnp.sqrt(omega_mean * omega_mean + strain / (LIMIT_A1 * LIMIT_A1))
    viscous = MU_LAMINAR + eddy_visc
    heating = viscous * lax.optimization_barrier(jnp.sum(0.5 * (centre[1:4] + opposite[1:4]) * velocity_jump, axis=0)) + KAPPA_HEAT * (opposite[4] / opposite[0] - centre[4] / centre[0])
    produce = 0.5 * eddy_visc * strain
    kinetic_flux = (MU_LAMINAR + SIGMA_K * eddy_visc) * (opposite[5] - centre[5]) + produce
    omega_flux = (MU_LAMINAR + SIGMA_OMEGA * eddy_visc) * (opposite[6] - centre[6]) + ALPHA_OMEGA * centre[6] / centre[5] * produce
    diffuse = jnp.stack([jnp.zeros_like(strain), viscous * velocity_jump[0], viscous * velocity_jump[1], viscous * velocity_jump[2], heating, kinetic_flux, omega_flux])
    return diffuse - convect

def source_term(cell_values):
    blank = jnp.zeros_like(cell_values[0])
    kinetic_sink = -BETA_STAR * cell_values[0] * cell_values[5] * cell_values[6]
    omega_sink = -BETA_OMEGA * cell_values[0] * cell_values[6] * cell_values[6]
    return jnp.stack([blank, blank, blank, blank, blank, kinetic_sink, omega_sink])

def block_residual(cell_values, ghosts, cell_kinds, farfield):
    before_i = jnp.concatenate([ghosts[0][:, None], cell_values[:, :-1]], axis=1)
    after_i = jnp.concatenate([cell_values[:, 1:], ghosts[1][:, None]], axis=1)
    before_j = jnp.concatenate([ghosts[2][:, :, None], cell_values[:, :, :-1]], axis=2)
    after_j = jnp.concatenate([cell_values[:, :, 1:], ghosts[3][:, :, None]], axis=2)
    before_k = jnp.roll(cell_values, 1, axis=3)
    after_k = jnp.roll(cell_values, -1, axis=3)
    summed = source_term(cell_values)
    summed = summed + pair_term(cell_values, before_i, 0, -1.0) + pair_term(cell_values, after_i, 0, 1.0)
    summed = summed + pair_term(cell_values, before_j, 1, -1.0) + pair_term(cell_values, after_j, 1, 1.0)
    summed = summed + pair_term(cell_values, before_k, 2, -1.0) + pair_term(cell_values, after_k, 2, 1.0)
    fluid = (cell_kinds != 1).astype(cell_values.dtype)
    sponge = (cell_kinds == 2).astype(cell_values.dtype)
    solid = (cell_kinds == 1).astype(cell_values.dtype)
    far_cell = farfield[:, None, None, None]
    resting = jnp.array([1.0, 0.0, 0.0, 0.0, 1.0, 1.0, 1.0], cell_values.dtype)[:, None, None, None] * far_cell
    return fluid * summed + DAMPING * sponge * (cell_values - far_cell) + solid * (cell_values - resting)

def reorient(values, turn_flags):
    swirl_signs = jnp.array([1.0, 1.0, 1.0, -1.0, 1.0, 1.0, 1.0], values.dtype)[:, None, None]
    turned = jnp.flip(values, axis=-1) * swirl_signs
    return jnp.where(turn_flags, turned, values)

def reference(flow_state, adjoint, cell_codes, block_links, farfield):
    face_layers = jnp.stack([flow_state[:, :, 0], flow_state[:, :, -1], flow_state[:, :, :, 0], flow_state[:, :, :, -1]], axis=1)
    partner = block_links[:, :, 0].astype(jnp.int32)
    turn_flags = (block_links[:, :, 1] == 1)[:, :, None, None, None]
    present = (partner >= 0)[:, :, None, None, None]
    facing = jnp.array([1, 0, 3, 2], jnp.int32)[None, :]
    source_block = jnp.maximum(partner, 0).astype(jnp.int32)
    partner_side = face_layers[source_block, facing]
    far_face = jnp.broadcast_to(farfield[:, None, None], face_layers.shape[2:])
    ghosts = jnp.where(present, reorient(partner_side, turn_flags), far_face)

    def per_block(block_items):
        cell_values, ghost_layers, cell_kinds, weights = block_items
        _, pullback = jax.vjp(lambda cells_arg, ghost_arg: block_residual(cells_arg, ghost_arg, cell_kinds, farfield), cell_values, ghost_layers)
        return pullback(weights)
    gradient, ghost_cot = lax.map(per_block, (flow_state, ghosts, cell_codes, adjoint))
    returned = jnp.where(present, reorient(ghost_cot, turn_flags), 0.0)
    landed = jnp.zeros_like(face_layers).at[source_block, facing].add(returned)
    gradient = gradient.at[:, :, 0].add(landed[:, 0])
    gradient = gradient.at[:, :, -1].add(landed[:, 1])
    gradient = gradient.at[:, :, :, 0].add(landed[:, 2])
    gradient = gradient.at[:, :, :, -1].add(landed[:, 3])
    return gradient
```

```python
import functools

import jax
import jax.numpy as jnp
from jax import lax
from jax.experimental import pallas as pl
from jax.experimental.pallas import tpu as pltpu
from jax.sharding import PartitionSpec as P

GAMMA = 1.4
MU_LAMINAR = 0.02
KAPPA_HEAT = 0.07
SIGMA_K = 0.85
SIGMA_OMEGA = 0.5
BETA_STAR = 0.09
BETA_OMEGA = 0.075
ALPHA_OMEGA = 0.52
INV_A1_SQ = 1.0 / (0.31 * 0.31)
DAMPING = 2.0

NV = 7
AXES = ("group", "block")
VMEM = pl.BlockSpec(memory_space=pltpu.VMEM)
SMEM = pl.BlockSpec(memory_space=pltpu.SMEM)
PARAMS = pltpu.CompilerParams(vmem_limit_bytes=24 << 20)


def prepare(state, weight):
    rho, u1, u2, u3, p, kt, om = state
    half_rho = 0.5 * rho
    cons = [
        rho,
        rho * u1,
        rho * u2,
        rho * u3,
        p * (1.0 / (GAMMA - 1.0)) + half_rho * (u1 * u1 + u2 * u2 + u3 * u3),
        rho * kt,
        rho * om,
    ]
    half_sound = 0.5 * jnp.sqrt(GAMMA * (p / rho))
    produce = weight[5] + (ALPHA_OMEGA * weight[6]) * (om / kt)
    return dict(s=state, m=weight, q=cons, h=half_sound, v=produce)


def moved(cell, shift):
    return dict(
        s=[shift(x) for x in cell["s"]],
        m=[shift(x) for x in cell["m"]],
        q=[shift(x) for x in cell["q"]],
        h=shift(cell["h"]),
        v=shift(cell["v"]),
    )


def sign(x):
    return jnp.where(x > 0.0, 1.0, jnp.where(x < 0.0, -1.0, 0.0))


def face_pair(low, high, axis, mask=None):
    n = 1 + axis
    sa, sc = low["s"], high["s"]
    delta = [c - a for a, c in zip(low["m"], high["m"])]
    weight_sum = low["v"] + high["v"]
    if mask is not None:
        delta = [jnp.where(mask, d, 0.0) for d in delta]
        weight_sum = jnp.where(mask, weight_sum, 0.0)
    qa = functools.reduce(jnp.add, [d * q for d, q in zip(delta, low["q"])])
    qc = functools.reduce(jnp.add, [d * q for d, q in zip(delta, high["q"])])
    half_wa, half_wc = 0.5 * sa[n], 0.5 * sc[n]
    half_lam = 0.5 * (jnp.abs(half_wa) + jnp.abs(half_wc) + low["h"] + high["h"])
    ca, cc = half_wa + half_lam, half_wc - half_lam
    slope = 0.5 * (qa - qc)

    e = [sc[i] - sa[i] for i in (1, 2, 3)]
    half_d4 = 0.5 * delta[4]
    g = [delta[i] + half_d4 * (sa[i] + sc[i]) for i in (1, 2, 3)]
    strain = e[0] * e[0] + e[1] * e[1] + e[2] * e[2]
    eg = e[0] * g[0] + e[1] * g[1] + e[2] * g[2]
    rho_m = 0.5 * (sa[0] + sc[0])
    kt_m = 0.5 * (sa[5] + sc[5])
    om_m = 0.5 * (sa[6] + sc[6])
    inv = lax.rsqrt(om_m * om_m + strain * INV_A1_SQ)
    mut = rho_m * kt_m * inv
    d_mut = (
        0.5 * (strain * weight_sum)
        - eg
        - SIGMA_K * (delta[5] * (sc[5] - sa[5]))
        - SIGMA_OMEGA * (delta[6] * (sc[6] - sa[6]))
    )
    nu = MU_LAMINAR + mut
    limited = d_mut * mut * (inv * inv)
    along = mut * weight_sum - limited * INV_A1_SQ
    k_flux = delta[5] * (MU_LAMINAR + SIGMA_K * mut)
    o_flux = delta[6] * (MU_LAMINAR + SIGMA_OMEGA * mut)
    half_inv = 0.5 * (d_mut * inv)
    k_mean = half_inv * rho_m
    rho_mean = half_inv * kt_m
    o_mean = -0.5 * (limited * om_m)
    heat = KAPPA_HEAT * delta[4]
    produced = 0.5 * (mut * strain)
    if mask is not None:
        produced = jnp.where(mask, produced, 0.0)
    side = nu * half_d4
    lower = [ca * d for d in delta]
    upper = [cc * d for d in delta]
    for i in range(3):
        jump = along * e[i] - nu * g[i]
        mean = side * e[i]
        low_u, high_u = -jump - mean, jump - mean
        if i == axis:
            low_u += 0.5 * (qa + sa[4] * delta[4]) + 0.5 * (slope * sign(sa[n]))
            high_u += 0.5 * (qc + sc[4] * delta[4]) + 0.5 * (slope * sign(sc[n]))
        lower.append(low_u)
        upper.append(high_u)
    half_dn = 0.5 * delta[n]
    lower += [half_dn + half_wa * delta[4], k_mean + k_flux, o_mean + o_flux]
    upper += [half_dn + half_wc * delta[4], k_mean - k_flux, o_mean - o_flux]
    lower += [rho_mean, heat, produced, slope]
    upper += [rho_mean, -heat, produced, slope]
    return lower, upper


def to_gradient(acc, cell):
    rho, u1, u2, u3, p, kt, om = cell["s"]
    inv_rho = 1.0 / rho
    inv_kt = 1.0 / kt
    half_wave = 0.5 * (acc[16] * cell["h"])
    heat = acc[14] * inv_rho
    y4 = acc[4]
    produced = ALPHA_OMEGA * (cell["m"][6] * acc[15]) * inv_kt
    d_rho = (
        acc[0]
        + acc[1] * u1
        + acc[2] * u2
        + acc[3] * u3
        + 0.5 * (y4 * (u1 * u1 + u2 * u2 + u3 * u3))
        + acc[5] * kt
        + acc[6] * om
        + acc[13]
        - (heat * p + half_wave) * inv_rho
    )
    return [
        d_rho,
        rho * (acc[1] + y4 * u1) + acc[7],
        rho * (acc[2] + y4 * u2) + acc[8],
        rho * (acc[3] + y4 * u3) + acc[9],
        y4 * (1.0 / (GAMMA - 1.0)) + acc[10] + heat + half_wave / p,
        rho * acc[5] + acc[11] - produced * (om * inv_kt),
        rho * acc[6] + acc[12] + produced,
    ]


def fluid_weight(code, adjoint):
    fluid = code != 1
    return [jnp.where(fluid, x, 0.0) for x in adjoint]


def pack_kernel(slots, links, flow, adj, codes, *outs):
    group, me = lax.axis_index("group"), lax.axis_index("block")
    peers = slots + 1

    def layer(rows):
        state = [flow[v, rows, :] for v in range(NV)]
        return state + fluid_weight(codes[rows, :], [adj[v, rows, :] for v in range(NV)])

    low, high = layer(pl.ds(0, 8, stride=8)), layer(pl.ds(7, 8, stride=8))
    up = links[6]
    goal_up = jnp.where(up >= 0, lax.rem(up, peers) ^ me, -1)
    for m in range(1, peers):
        upward = goal_up == m
        for v in range(2 * NV):
            outs[m - 1][v] = jnp.where(upward, high[v], low[v])
    even = lax.rem(group, 2) == 0
    for t in range(2):
        upper = even if t == 0 else jnp.logical_not(even)
        row = pl.multiple_of(jnp.where(upper, 56, 0), 8)
        values = layer(pl.ds(row, 8))
        partner = jnp.where(upper, links[2], links[0])
        goal = jnp.where(partner >= 0, lax.rem(partner, peers), -1)
        for v in range(2 * NV):
            outs[slots][t, v] = values[v]
        outs[slots][t, 2 * NV] = jnp.full((8, 128), goal.astype(jnp.float32))


def relay_kernel(near, far, *refs):
    me = lax.axis_index("block")
    sources, outs = refs[:near], refs[near:]
    for t in range(2):
        goals = [src[t, 2 * NV] for src in sources]
        for q in range(far):
            wanted = (me ^ (q * near)).astype(jnp.float32)
            masks = [goal == wanted for goal in goals]
            for v in range(2 * NV):
                value = sources[0][t, v]
                for src, mask in zip(sources[1:], masks[1:]):
                    value = jnp.where(mask, src[t, v], value)
                outs[t * far + q][v] = value


def interior_kernel(flow, adj, codes, out, carry):
    sublane = lax.broadcasted_iota(jnp.int32, (8, 128), 0)
    inside = sublane < 7

    def load(i):
        rows = pl.ds(pl.multiple_of(i * 8, 8), 8)
        raw = [adj[v, rows, :] for v in range(NV)]
        code = codes[rows, :]
        state = [flow[v, rows, :] for v in range(NV)]
        return prepare(state, fluid_weight(code, raw)), raw, code, rows

    carry[...] = jnp.zeros_like(carry)

    def step(i, _):
        cell, raw, code, rows = load(i)
        acc = [carry[n] for n in range(17)]
        for axis, dim, size, mask in ((2, 1, 128, None), (1, 0, 8, inside)):
            after = moved(cell, lambda x: pltpu.roll(x, size - 1, dim))
            lower, upper = face_pair(cell, after, axis, mask)
            acc = [t + lo + pltpu.roll(hi, 1, dim) for t, lo, hi in zip(acc, lower, upper)]

        def emit(acc):
            grad = to_gradient(acc, cell)
            rho, kt, om = cell["s"][0], cell["s"][5], cell["s"][6]
            w5, w6 = BETA_STAR * cell["m"][5], BETA_OMEGA * cell["m"][6]
            grad[0] -= (w5 * kt + w6 * om) * om
            grad[5] -= w5 * rho * om
            grad[6] -= (w5 * kt + 2.0 * w6 * om) * rho
            local = jnp.where(code == 2, DAMPING, jnp.where(code == 1, 1.0, 0.0))
            for v in range(NV):
                out[v, rows, :] = grad[v] + local * raw[v]

        @pl.when(i < 7)
        def _():
            lower, upper = face_pair(cell, load(i + 1)[0], 0)
            for n in range(17):
                carry[n] = upper[n]
            emit([t + lo for t, lo in zip(acc, lower)])

        @pl.when(i == 7)
        def _():
            emit(acc)

        return 0

    lax.fori_loop(0, 8, step, 0)


def rim_kernel(slots, far, near, links, farfield, grad, flow, adj, codes, *refs):
    radial, axial = refs[:slots], refs[slots : slots + 2 * far]
    out, ghost = refs[slots + 2 * far :]
    group, me = lax.axis_index("group"), lax.axis_index("block")
    peers = slots + 1
    even = lax.rem(group, 2) == 0
    out[...] = grad[...]
    lane = lax.broadcasted_iota(jnp.int32, (8, 128), 1)
    for face in range(4):
        partner, turned = links[2 * face], links[2 * face + 1] == 1
        present = partner >= 0
        offset = lax.rem(jnp.maximum(partner, 0), peers) ^ me

        def fetch(source):
            for v in range(2 * NV):
                ghost[v] = source[v]

        @pl.when(jnp.logical_not(present))
        def _():
            for v in range(NV):
                ghost[v] = jnp.full((8, 128), farfield[v])
                ghost[NV + v] = jnp.zeros((8, 128), jnp.float32)

        if face < 2:
            first = even if face == 1 else jnp.logical_not(even)
            for q in range(far):
                here = present & (offset // near == q)
                pl.when(here & first)(functools.partial(fetch, axial[q]))
                pl.when(here & jnp.logical_not(first))(functools.partial(fetch, axial[far + q]))
        else:
            for m in range(1, peers):
                pl.when(present & (offset == m))(functools.partial(fetch, radial[m - 1]))
        index = jnp.where(turned, 127 - lane, lane)
        values = [jnp.take_along_axis(ghost[v], index, axis=1) for v in range(2 * NV)]
        swirl = jnp.where(turned, -1.0, 1.0)
        for v in (3, NV + 3):
            values[v] = values[v] * swirl
        other = prepare(values[:NV], values[NV:])
        rows = (pl.ds(0, 8), pl.ds(56, 8), pl.ds(0, 8, stride=8), pl.ds(7, 8, stride=8))[face]
        state = [flow[v, rows, :] for v in range(NV)]
        weight = fluid_weight(codes[rows, :], [adj[v, rows, :] for v in range(NV)])
        cell = prepare(state, weight)
        if face % 2 == 0:
            acc = face_pair(other, cell, face // 2)[1]
        else:
            acc = face_pair(cell, other, face // 2)[0]
        for v, value in enumerate(to_gradient(acc, cell)):
            out[v, rows, :] = out[v, rows, :] + value


def shape(*dims):
    return jax.ShapeDtypeStruct(dims, jnp.float32)


def solution(mesh):
    groups, peers = mesh.shape["group"], mesh.shape["block"]
    bits = peers.bit_length() - 1
    near = 1 << ((bits + 1) // 2)
    far = peers // near
    slots = peers - 1

    def within(offset):
        return [
            (g * peers + h, g * peers + (h ^ offset)) for g in range(groups) for h in range(peers)
        ]

    def between(first, offset):
        pairs = []
        for g in range(groups):
            other = g + 1 if (g % 2 == 0) == first else g - 1
            if 0 <= other < groups:
                pairs += [(g * peers + h, other * peers + (h ^ offset)) for h in range(peers)]
        return pairs

    def per_device(flow_state, adjoint, cell_codes, block_links, farfield):
        flow = flow_state.reshape(NV, 64, 128)
        adj = adjoint.reshape(NV, 64, 128)
        codes = cell_codes.reshape(64, 128)
        links = block_links.reshape(8)
        packed = pl.pallas_call(
            functools.partial(pack_kernel, slots),
            out_shape=[shape(2 * NV, 8, 128)] * slots + [shape(2, 2 * NV + 1, 8, 128)],
            in_specs=[SMEM, VMEM, VMEM, VMEM],
            out_specs=[VMEM] * (slots + 1),
            compiler_params=PARAMS,
            name="pack",
        )(links, flow, adj, codes)
        pair = packed[slots]
        sources = [pair] + [lax.ppermute(pair, AXES, within(o)) for o in range(1, near)]
        radial = [lax.ppermute(packed[m - 1], AXES, within(m)) for m in range(1, peers)]
        relayed = pl.pallas_call(
            functools.partial(relay_kernel, near, far),
            out_shape=[shape(2 * NV, 8, 128)] * (2 * far),
            in_specs=[VMEM] * near,
            out_specs=[VMEM] * (2 * far),
            compiler_params=PARAMS,
            name="relay",
        )(*sources)
        axial = [
            lax.ppermute(relayed[t * far + q], AXES, between(t == 0, q * near))
            for t in range(2)
            for q in range(far)
        ]
        inner = pl.pallas_call(
            interior_kernel,
            out_shape=shape(NV, 64, 128),
            in_specs=[VMEM] * 3,
            out_specs=VMEM,
            scratch_shapes=[pltpu.VMEM((17, 8, 128), jnp.float32)],
            compiler_params=PARAMS,
            cost_estimate=pl.CostEstimate(flops=6000000, bytes_accessed=800000, transcendentals=60000),
            name="interior",
        )(flow, adj, codes)
        result = pl.pallas_call(
            functools.partial(rim_kernel, slots, far, near),
            out_shape=shape(NV, 64, 128),
            in_specs=[SMEM, SMEM] + [VMEM] * (4 + slots + 2 * far),
            out_specs=VMEM,
            scratch_shapes=[pltpu.VMEM((2 * NV, 8, 128), jnp.float32)],
            compiler_params=PARAMS,
            name="rim",
        )(links, farfield, inner, flow, adj, codes, *radial, *axial)
        return result.reshape(flow_state.shape)

    spec = P(("group", "block"), None, None, None, None)
    return jax.shard_map(
        per_device,
        mesh=mesh,
        in_specs=(
            spec,
            spec,
            P(("group", "block"), None, None, None),
            P(("group", "block"), None, None),
            P(),
        ),
        out_specs=spec,
        check_vma=False,
    )
```

```python
import functools

import jax
import jax.numpy as jnp
from jax import lax
from jax.experimental import pallas as pl
from jax.experimental.pallas import tpu as pltpu
from jax.sharding import PartitionSpec as P

GAMMA = 1.4
MU_LAMINAR = 0.02
KAPPA_HEAT = 0.07
SIGMA_K = 0.85
SIGMA_OMEGA = 0.5
BETA_STAR = 0.09
BETA_OMEGA = 0.075
ALPHA_OMEGA = 0.52
INV_A1_SQ = 1.0 / (0.31 * 0.31)
DAMPING = 2.0

NV = 7
AXES = ("group", "block")
VMEM = pl.BlockSpec(memory_space=pltpu.VMEM)
SMEM = pl.BlockSpec(memory_space=pltpu.SMEM)
PARAMS = pltpu.CompilerParams(vmem_limit_bytes=24 << 20)


def prepare(state, weight):
    rho, u1, u2, u3, p, kt, om = state
    half_rho = 0.5 * rho
    cons = [
        rho,
        rho * u1,
        rho * u2,
        rho * u3,
        p * (1.0 / (GAMMA - 1.0)) + half_rho * (u1 * u1 + u2 * u2 + u3 * u3),
        rho * kt,
        rho * om,
    ]
    half_sound = 0.5 * jnp.sqrt(GAMMA * (p / rho))
    produce = weight[5] + (ALPHA_OMEGA * weight[6]) * (om / kt)
    return dict(s=state, m=weight, q=cons, h=half_sound, v=produce)


def moved(cell, shift):
    return dict(
        s=[shift(x) for x in cell["s"]],
        m=[shift(x) for x in cell["m"]],
        q=[shift(x) for x in cell["q"]],
        h=shift(cell["h"]),
        v=shift(cell["v"]),
    )


def sign(x):
    return jnp.where(x > 0.0, 1.0, jnp.where(x < 0.0, -1.0, 0.0))


def face_pair(low, high, axis, mask=None):
    n = 1 + axis
    sa, sc = low["s"], high["s"]
    delta = [c - a for a, c in zip(low["m"], high["m"])]
    weight_sum = low["v"] + high["v"]
    if mask is not None:
        delta = [jnp.where(mask, d, 0.0) for d in delta]
        weight_sum = jnp.where(mask, weight_sum, 0.0)
    qa = functools.reduce(jnp.add, [d * q for d, q in zip(delta, low["q"])])
    qc = functools.reduce(jnp.add, [d * q for d, q in zip(delta, high["q"])])
    half_wa, half_wc = 0.5 * sa[n], 0.5 * sc[n]
    half_lam = 0.5 * (jnp.abs(half_wa) + jnp.abs(half_wc) + low["h"] + high["h"])
    ca, cc = half_wa + half_lam, half_wc - half_lam
    slope = 0.5 * (qa - qc)

    e = [sc[i] - sa[i] for i in (1, 2, 3)]
    half_d4 = 0.5 * delta[4]
    g = [delta[i] + half_d4 * (sa[i] + sc[i]) for i in (1, 2, 3)]
    strain = e[0] * e[0] + e[1] * e[1] + e[2] * e[2]
    eg = e[0] * g[0] + e[1] * g[1] + e[2] * g[2]
    rho_m = 0.5 * (sa[0] + sc[0])
    kt_m = 0.5 * (sa[5] + sc[5])
    om_m = 0.5 * (sa[6] + sc[6])
    inv = lax.rsqrt(om_m * om_m + strain * INV_A1_SQ)
    mut = rho_m * kt_m * inv
    d_mut = (
        0.5 * (strain * weight_sum)
        - eg
        - SIGMA_K * (delta[5] * (sc[5] - sa[5]))
        - SIGMA_OMEGA * (delta[6] * (sc[6] - sa[6]))
    )
    nu = MU_LAMINAR + mut
    limited = d_mut * mut * (inv * inv)
    along = mut * weight_sum - limited * INV_A1_SQ
    k_flux = delta[5] * (MU_LAMINAR + SIGMA_K * mut)
    o_flux = delta[6] * (MU_LAMINAR + SIGMA_OMEGA * mut)
    half_inv = 0.5 * (d_mut * inv)
    k_mean = half_inv * rho_m
    rho_mean = half_inv * kt_m
    o_mean = -0.5 * (limited * om_m)
    heat = KAPPA_HEAT * delta[4]
    produced = 0.5 * (mut * strain)
    if mask is not None:
        produced = jnp.where(mask, produced, 0.0)
    side = nu * half_d4
    lower = [ca * d for d in delta]
    upper = [cc * d for d in delta]
    for i in range(3):
        jump = along * e[i] - nu * g[i]
        mean = side * e[i]
        low_u, high_u = -jump - mean, jump - mean
        if i == axis:
            low_u += 0.5 * (qa + sa[4] * delta[4]) + 0.5 * (slope * sign(sa[n]))
            high_u += 0.5 * (qc + sc[4] * delta[4]) + 0.5 * (slope * sign(sc[n]))
        lower.append(low_u)
        upper.append(high_u)
    half_dn = 0.5 * delta[n]
    lower += [half_dn + half_wa * delta[4], k_mean + k_flux, o_mean + o_flux]
    upper += [half_dn + half_wc * delta[4], k_mean - k_flux, o_mean - o_flux]
    lower += [rho_mean, heat, produced, slope]
    upper += [rho_mean, -heat, produced, slope]
    return lower, upper


def to_gradient(acc, cell):
    rho, u1, u2, u3, p, kt, om = cell["s"]
    inv_rho = 1.0 / rho
    inv_kt = 1.0 / kt
    half_wave = 0.5 * (acc[16] * cell["h"])
    heat = acc[14] * inv_rho
    y4 = acc[4]
    produced = ALPHA_OMEGA * (cell["m"][6] * acc[15]) * inv_kt
    d_rho = (
        acc[0]
        + acc[1] * u1
        + acc[2] * u2
        + acc[3] * u3
        + 0.5 * (y4 * (u1 * u1 + u2 * u2 + u3 * u3))
        + acc[5] * kt
        + acc[6] * om
        + acc[13]
        - (heat * p + half_wave) * inv_rho
    )
    return [
        d_rho,
        rho * (acc[1] + y4 * u1) + acc[7],
        rho * (acc[2] + y4 * u2) + acc[8],
        rho * (acc[3] + y4 * u3) + acc[9],
        y4 * (1.0 / (GAMMA - 1.0)) + acc[10] + heat + half_wave / p,
        rho * acc[5] + acc[11] - produced * (om * inv_kt),
        rho * acc[6] + acc[12] + produced,
    ]


def fluid_weight(code, adjoint):
    fluid = code != 1
    return [jnp.where(fluid, x, 0.0) for x in adjoint]


def pack_kernel(peers, links, flow_in, adj_in, codes_in, flow, adj, codes, radial, even_pair, odd_pair, sems):
    group = lax.axis_index("group")
    copies = []
    for v in range(NV):
        copies.append(pltpu.make_async_copy(flow_in.at[v], flow.at[v], sems.at[v]))
        copies.append(pltpu.make_async_copy(adj_in.at[v], adj.at[v], sems.at[NV + v]))
    copies.append(pltpu.make_async_copy(codes_in, codes, sems.at[2 * NV]))
    for copy in copies:
        copy.start()
    for copy in copies:
        copy.wait()

    def layer(out, rows, partner):
        for v in range(NV):
            out[v] = flow[v, rows, :]
        fluid = codes[rows, :] != 1
        for v in range(NV):
            out[NV + v] = jnp.where(fluid, adj[v, rows, :], 0.0)
        goal = jnp.where(partner >= 0, lax.rem(partner, peers), -1)
        out[2 * NV] = jnp.full((8, 128), goal.astype(jnp.float32))

    layer(radial.at[0], pl.ds(0, 8, stride=8), links[0, 2])
    layer(radial.at[1], pl.ds(7, 8, stride=8), links[0, 3])
    even = lax.rem(group, 2) == 0
    for out, upper in ((even_pair, even), (odd_pair, jnp.logical_not(even))):
        row = pl.multiple_of(jnp.where(upper, 56, 0), 8)
        layer(out.at[0], pl.ds(row, 8), jnp.where(upper, links[0, 1], links[0, 0]))


def relay_kernel(offsets, sources, *refs):
    me = lax.axis_index("block")
    arrays, outs = refs[: -len(offsets)], refs[-len(offsets) :]
    for t, places in enumerate(sources):
        held = [arrays[at].at[k] for at, k in places]
        goals = [x[2 * NV] for x in held[1:]]
        for out, offset in zip(outs, offsets):
            wanted = (me ^ offset).astype(jnp.float32)
            masks = [goal == wanted for goal in goals]
            for v in range(2 * NV):
                value = held[0][v]
                for x, mask in zip(held[1:], masks):
                    value = jnp.where(mask, x[v], value)
                out[t, v] = value


def interior_kernel(flow, adj, codes, out, carry):
    sublane = lax.broadcasted_iota(jnp.int32, (8, 128), 0)
    inside = sublane < 7

    def load(i):
        rows = pl.ds(pl.multiple_of(i * 8, 8), 8)
        raw = [adj[v, rows, :] for v in range(NV)]
        code = codes[rows, :]
        state = [flow[v, rows, :] for v in range(NV)]
        return prepare(state, fluid_weight(code, raw)), raw, code, rows

    carry[...] = jnp.zeros_like(carry)

    def step(i, _):
        cell, raw, code, rows = load(i)
        acc = [carry[n] for n in range(17)]
        for axis, dim, size, mask in ((2, 1, 128, None), (1, 0, 8, inside)):
            after = moved(cell, lambda x: pltpu.roll(x, size - 1, dim))
            lower, upper = face_pair(cell, after, axis, mask)
            acc = [t + lo + pltpu.roll(hi, 1, dim) for t, lo, hi in zip(acc, lower, upper)]

        def emit(acc):
            grad = to_gradient(acc, cell)
            rho, kt, om = cell["s"][0], cell["s"][5], cell["s"][6]
            w5, w6 = BETA_STAR * cell["m"][5], BETA_OMEGA * cell["m"][6]
            grad[0] -= (w5 * kt + w6 * om) * om
            grad[5] -= w5 * rho * om
            grad[6] -= (w5 * kt + 2.0 * w6 * om) * rho
            local = jnp.where(code == 2, DAMPING, jnp.where(code == 1, 1.0, 0.0))
            for v in range(NV):
                out[v, rows, :] = grad[v] + local * raw[v]

        @pl.when(i < 7)
        def _():
            lower, upper = face_pair(cell, load(i + 1)[0], 0)
            for n in range(17):
                carry[n] = upper[n]
            emit([t + lo for t, lo in zip(acc, lower)])

        @pl.when(i == 7)
        def _():
            emit(acc)

        return 0

    lax.fori_loop(0, 8, step, 0)


def rim_kernel(peers, plans, links, farfield, grad, flow, adj, codes, *refs):
    arrays, (out, ghost) = refs[:-2], refs[-2:]
    group, me = lax.axis_index("group"), lax.axis_index("block")
    even = lax.rem(group, 2) == 0
    out[...] = grad[...]
    lane = lax.broadcasted_iota(jnp.int32, (8, 128), 1)
    for face in range(4):
        partner, turned = links[0, face], links[1, face] == 1
        present = partner >= 0
        offset = lax.rem(jnp.maximum(partner, 0), peers) ^ me

        def fetch(source, t):
            for v in range(2 * NV):
                ghost[v] = source[t, v]

        @pl.when(jnp.logical_not(present))
        def _():
            for v in range(NV):
                ghost[v] = jnp.full((8, 128), farfield[v])
                ghost[NV + v] = jnp.zeros((8, 128), jnp.float32)

        if face < 2:
            first = even if face == 1 else jnp.logical_not(even)
            choices = [("even", present & first), ("odd", present & jnp.logical_not(first))]
        else:
            choices = [("high" if face == 2 else "low", present)]
        for kind, chosen in choices:
            for step, (at, t) in plans[kind].items():
                pl.when(chosen & (offset == step))(functools.partial(fetch, arrays[at], t))
        index = jnp.where(turned, 127 - lane, lane)
        values = [jnp.take_along_axis(ghost[v], index, axis=1) for v in range(2 * NV)]
        swirl = jnp.where(turned, -1.0, 1.0)
        for v in (3, NV + 3):
            values[v] = values[v] * swirl
        other = prepare(values[:NV], values[NV:])
        rows = (pl.ds(0, 8), pl.ds(56, 8), pl.ds(0, 8, stride=8), pl.ds(7, 8, stride=8))[face]
        state = [flow[v, rows, :] for v in range(NV)]
        weight = fluid_weight(codes[rows, :], [adj[v, rows, :] for v in range(NV)])
        cell = prepare(state, weight)
        if face % 2 == 0:
            acc = face_pair(other, cell, face // 2)[1]
        else:
            acc = face_pair(cell, other, face // 2)[0]
        for v, value in enumerate(to_gradient(acc, cell)):
            out[v, rows, :] = out[v, rows, :] + value


def shape(*dims, dtype=jnp.float32):
    return jax.ShapeDtypeStruct(dims, dtype)


def span(basis):
    offsets = [0]
    for b in basis:
        offsets += [o ^ b for o in offsets]
    return offsets


def solution(mesh):
    groups, peers = mesh.shape["group"], mesh.shape["block"]
    bits = peers.bit_length() - 1
    basis = [1 << i for i in range(bits - 1)] + [peers - 2]

    def within(offset):
        return [
            (g * peers + h, g * peers + (h ^ offset)) for g in range(groups) for h in range(peers)
        ]

    def between(first, offset):
        pairs = []
        for g in range(groups):
            other = (g + 1 if (g % 2 == 0) == first else g - 1) % groups
            pairs += [(g * peers + h, other * peers + (h ^ offset)) for h in range(peers)]
        return pairs

    def relay(offsets, sources):
        arrays = []
        for x, _ in sum(sources, []):
            if not any(x is y for y in arrays):
                arrays.append(x)
        places = [[(next(n for n, y in enumerate(arrays) if y is x), k) for x, k in held] for held in sources]
        return pl.pallas_call(
            functools.partial(relay_kernel, offsets, places),
            out_shape=[shape(len(sources), 2 * NV, 8, 128)] * len(offsets),
            in_specs=[VMEM] * len(arrays),
            out_specs=[VMEM] * len(offsets),
            compiler_params=PARAMS,
            name="relay",
        )(*arrays)

    near, far = span(basis[: (bits + 1) // 2]), span(basis[(bits + 1) // 2 :])

    def per_device(flow_state, adjoint, cell_codes, block_links, farfield):
        links = jnp.transpose(block_links[0])
        whole = flow_state.reshape(NV, 64, 128), adjoint.reshape(NV, 64, 128), cell_codes.reshape(64, 128)
        flow, adj, codes, radial, even_pair, odd_pair = pl.pallas_call(
            functools.partial(pack_kernel, peers),
            out_shape=[
                shape(NV, 64, 128),
                shape(NV, 64, 128),
                shape(64, 128, dtype=jnp.int32),
                shape(2, 2 * NV + 1, 8, 128),
                shape(1, 2 * NV + 1, 8, 128),
                shape(1, 2 * NV + 1, 8, 128),
            ],
            in_specs=[SMEM] + [pl.BlockSpec(memory_space=pltpu.HBM)] * 3,
            out_specs=[VMEM] * 6,
            scratch_shapes=[pltpu.SemaphoreType.DMA((2 * NV + 1,))],
            compiler_params=PARAMS,
            name="pack",
        )(links, *[pltpu.with_memory_space_constraint(x, pltpu.HBM) for x in whole])
        inner = pl.pallas_call(
            interior_kernel,
            out_shape=shape(NV, 64, 128),
            in_specs=[VMEM] * 3,
            out_specs=VMEM,
            scratch_shapes=[pltpu.VMEM((17, 8, 128), jnp.float32)],
            compiler_params=PARAMS,
            cost_estimate=pl.CostEstimate(flops=6000000, bytes_accessed=800000, transcendentals=60000),
            name="interior",
        )(flow, adj, codes)
        pair = jnp.concatenate(
            [lax.ppermute(even_pair, AXES, between(True, 0)), lax.ppermute(odd_pair, AXES, between(False, 0))]
        )
        held = {0: radial}
        for b in basis[: (bits + 1) // 2]:
            for o in list(held):
                held[o ^ b] = lax.ppermute(held[o], AXES, within(b))
        crossed = {o: lax.ppermute(pair, AXES, within(o)) if o else pair for o in far}
        inner, crossed = lax.optimization_barrier((inner, crossed))
        onward = relay(near[1:], [[(x, t) for x in crossed.values()] for t in range(2)])
        axial = {o: lax.ppermute(x, AXES, within(o)) for o, x in zip(near[1:], onward)}
        onward = relay(far[1:], [[(x, t) for x in held.values()] for t in range(2)])
        sent = {o: lax.ppermute(x, AXES, within(o)) for o, x in zip(far[1:], onward)}
        arrays, plans = [], dict(even={}, odd={}, low={}, high={})

        def place(kind, step, x, t):
            at = next((n for n, y in enumerate(arrays) if y is x), len(arrays))
            if at == len(arrays):
                arrays.append(x)
            plans[kind][step] = (at, t)

        for n in near:
            for f in far:
                for t in range(2):
                    x = axial[n] if n else crossed[f]
                    place(("even", "odd")[t], n ^ f, x, t)
                    x = sent[f] if f else held[n]
                    place(("low", "high")[t], n ^ f, x, t)
        result = pl.pallas_call(
            functools.partial(rim_kernel, peers, plans),
            out_shape=shape(NV, 64, 128),
            in_specs=[SMEM, SMEM] + [VMEM] * (4 + len(arrays)),
            out_specs=VMEM,
            scratch_shapes=[pltpu.VMEM((2 * NV, 8, 128), jnp.float32)],
            compiler_params=PARAMS,
            name="rim",
        )(links, farfield, inner, flow, adj, codes, *arrays)
        return result.reshape(flow_state.shape)

    spec = P(("group", "block"), None, None, None, None)
    return jax.shard_map(
        per_device,
        mesh=mesh,
        in_specs=(
            spec,
            spec,
            P(("group", "block"), None, None, None),
            P(("group", "block"), None, None),
            P(),
        ),
        out_specs=spec,
        check_vma=False,
    )
```

```python
import functools

import jax
import jax.numpy as jnp
from jax import lax
from jax.experimental import pallas as pl
from jax.experimental.pallas import tpu as pltpu
from jax.sharding import PartitionSpec as P

GAMMA = 1.4
MU_LAMINAR = 0.02
KAPPA_HEAT = 0.07
SIGMA_K = 0.85
SIGMA_OMEGA = 0.5
BETA_STAR = 0.09
BETA_OMEGA = 0.075
ALPHA_OMEGA = 0.52
INV_A1_SQ = 1.0 / (0.31 * 0.31)
DAMPING = 2.0

NV = 7
AXES = ("group", "block")
VMEM = pl.BlockSpec(memory_space=pltpu.VMEM)
SMEM = pl.BlockSpec(memory_space=pltpu.SMEM)
PARAMS = pltpu.CompilerParams(vmem_limit_bytes=24 << 20)


def prepare(state, weight):
    rho, u1, u2, u3, p, kt, om = state
    half_rho = 0.5 * rho
    cons = [
        rho,
        rho * u1,
        rho * u2,
        rho * u3,
        p * (1.0 / (GAMMA - 1.0)) + half_rho * (u1 * u1 + u2 * u2 + u3 * u3),
        rho * kt,
        rho * om,
    ]
    half_sound = 0.5 * jnp.sqrt(GAMMA * (p / rho))
    produce = weight[5] + (ALPHA_OMEGA * weight[6]) * (om / kt)
    return dict(s=state, m=weight, q=cons, h=half_sound, v=produce)


def moved(cell, shift):
    return dict(
        s=[shift(x) for x in cell["s"]],
        m=[shift(x) for x in cell["m"]],
        q=[shift(x) for x in cell["q"]],
        h=shift(cell["h"]),
        v=shift(cell["v"]),
    )


def sign(x):
    return jnp.where(x > 0.0, 1.0, jnp.where(x < 0.0, -1.0, 0.0))


def face_pair(low, high, axis, mask=None):
    n = 1 + axis
    sa, sc = low["s"], high["s"]
    delta = [c - a for a, c in zip(low["m"], high["m"])]
    weight_sum = low["v"] + high["v"]
    if mask is not None:
        delta = [jnp.where(mask, d, 0.0) for d in delta]
        weight_sum = jnp.where(mask, weight_sum, 0.0)
    qa = functools.reduce(jnp.add, [d * q for d, q in zip(delta, low["q"])])
    qc = functools.reduce(jnp.add, [d * q for d, q in zip(delta, high["q"])])
    half_wa, half_wc = 0.5 * sa[n], 0.5 * sc[n]
    half_lam = 0.5 * (jnp.abs(half_wa) + jnp.abs(half_wc) + low["h"] + high["h"])
    ca, cc = half_wa + half_lam, half_wc - half_lam
    slope = 0.5 * (qa - qc)

    e = [sc[i] - sa[i] for i in (1, 2, 3)]
    half_d4 = 0.5 * delta[4]
    g = [delta[i] + half_d4 * (sa[i] + sc[i]) for i in (1, 2, 3)]
    strain = e[0] * e[0] + e[1] * e[1] + e[2] * e[2]
    eg = e[0] * g[0] + e[1] * g[1] + e[2] * g[2]
    rho_m = 0.5 * (sa[0] + sc[0])
    kt_m = 0.5 * (sa[5] + sc[5])
    om_m = 0.5 * (sa[6] + sc[6])
    inv = lax.rsqrt(om_m * om_m + strain * INV_A1_SQ)
    mut = rho_m * kt_m * inv
    d_mut = (
        0.5 * (strain * weight_sum)
        - eg
        - SIGMA_K * (delta[5] * (sc[5] - sa[5]))
        - SIGMA_OMEGA * (delta[6] * (sc[6] - sa[6]))
    )
    nu = MU_LAMINAR + mut
    limited = d_mut * mut * (inv * inv)
    along = mut * weight_sum - limited * INV_A1_SQ
    k_flux = delta[5] * (MU_LAMINAR + SIGMA_K * mut)
    o_flux = delta[6] * (MU_LAMINAR + SIGMA_OMEGA * mut)
    half_inv = 0.5 * (d_mut * inv)
    k_mean = half_inv * rho_m
    rho_mean = half_inv * kt_m
    o_mean = -0.5 * (limited * om_m)
    heat = KAPPA_HEAT * delta[4]
    produced = 0.5 * (mut * strain)
    if mask is not None:
        produced = jnp.where(mask, produced, 0.0)
    side = nu * half_d4
    lower = [ca * d for d in delta]
    upper = [cc * d for d in delta]
    for i in range(3):
        jump = along * e[i] - nu * g[i]
        mean = side * e[i]
        low_u, high_u = -jump - mean, jump - mean
        if i == axis:
            low_u += 0.5 * (qa + sa[4] * delta[4]) + 0.5 * (slope * sign(sa[n]))
            high_u += 0.5 * (qc + sc[4] * delta[4]) + 0.5 * (slope * sign(sc[n]))
        lower.append(low_u)
        upper.append(high_u)
    half_dn = 0.5 * delta[n]
    lower += [half_dn + half_wa * delta[4], k_mean + k_flux, o_mean + o_flux]
    upper += [half_dn + half_wc * delta[4], k_mean - k_flux, o_mean - o_flux]
    lower += [rho_mean, heat, produced, slope]
    upper += [rho_mean, -heat, produced, slope]
    return lower, upper


def to_gradient(acc, cell):
    rho, u1, u2, u3, p, kt, om = cell["s"]
    inv_rho = 1.0 / rho
    inv_kt = 1.0 / kt
    half_wave = 0.5 * (acc[16] * cell["h"])
    heat = acc[14] * inv_rho
    y4 = acc[4]
    produced = ALPHA_OMEGA * (cell["m"][6] * acc[15]) * inv_kt
    d_rho = (
        acc[0]
        + acc[1] * u1
        + acc[2] * u2
        + acc[3] * u3
        + 0.5 * (y4 * (u1 * u1 + u2 * u2 + u3 * u3))
        + acc[5] * kt
        + acc[6] * om
        + acc[13]
        - (heat * p + half_wave) * inv_rho
    )
    return [
        d_rho,
        rho * (acc[1] + y4 * u1) + acc[7],
        rho * (acc[2] + y4 * u2) + acc[8],
        rho * (acc[3] + y4 * u3) + acc[9],
        y4 * (1.0 / (GAMMA - 1.0)) + acc[10] + heat + half_wave / p,
        rho * acc[5] + acc[11] - produced * (om * inv_kt),
        rho * acc[6] + acc[12] + produced,
    ]


def fluid_weight(code, adjoint):
    fluid = code != 1
    return [jnp.where(fluid, x, 0.0) for x in adjoint]


def pack_kernel(
    peers, links_in, farfield_in, flow_in, adj_in, codes_in, radial, pair, marks, far, links, farfield, states, weights, kinds, sems
):
    group, me = lax.axis_index("group"), lax.axis_index("block")
    copies = [pltpu.make_async_copy(links_in, links, sems.at[0]), pltpu.make_async_copy(farfield_in, farfield, sems.at[13])]
    for n, row in enumerate((0, 7)):
        copies.append(pltpu.make_async_copy(flow_in.at[:, :, row, :], states.at[n], sems.at[6 * n + 1]))
        copies.append(pltpu.make_async_copy(adj_in.at[:, :, row, :], weights.at[n], sems.at[6 * n + 2]))
        copies.append(pltpu.make_async_copy(codes_in.at[:, row, :], kinds.at[n], sems.at[6 * n + 3]))
        copies.append(pltpu.make_async_copy(flow_in.at[:, row], states.at[2 + n], sems.at[6 * n + 4]))
        copies.append(pltpu.make_async_copy(adj_in.at[:, row], weights.at[2 + n], sems.at[6 * n + 5]))
        copies.append(pltpu.make_async_copy(codes_in.at[row], kinds.at[2 + n], sems.at[6 * n + 6]))
    for copy in copies:
        copy.start()
    for copy in copies:
        copy.wait()

    def layer(out, n, partner):
        for v in range(NV):
            out[v] = states[n, v]
        fluid = kinds[n] != 1
        for v in range(NV):
            out[NV + v] = jnp.where(fluid, weights[n, v], 0.0)
        goal = jnp.where(partner >= 0, lax.rem(partner, peers), -1)
        out[2 * NV] = jnp.full((8, 128), goal.astype(jnp.float32))

    layer(radial.at[0], 0, links[0, 2])
    layer(radial.at[1], 1, links[0, 3])
    even = lax.rem(group, 2) == 0
    for t, upper in enumerate((even, jnp.logical_not(even))):
        layer(pair.at[t], jnp.where(upper, 3, 2), jnp.where(upper, links[0, 1], links[0, 0]))
    for face in range(4):
        partner = links[0, face]
        if face < 2:
            source = jnp.where(even, 1 - face, face)
        else:
            source = lax.rem(jnp.maximum(partner, 0), peers) ^ me
        marks[face] = jnp.full((8, 128), jnp.where(partner >= 0, source, -1))
        marks[4 + face] = jnp.full((8, 128), links[1, face])
    for v in range(NV):
        far[v] = jnp.full((8, 128), farfield[v])


def relay_kernel(offsets, sources, outs_of, *refs):
    me = lax.axis_index("block")
    for t, places in enumerate(sources):
        held = [refs[at].at[k] for at, k in places]
        goals = [x[2 * NV] for x in held]
        for offset, outs in zip(offsets, outs_of):
            wanted = (me ^ offset).astype(jnp.float32)
            masks = [goal == wanted for goal in goals]
            at, k = outs[t]
            out = refs[at]
            for v in range(out.shape[1]):
                value = held[0][v]
                for x, mask in zip(held[1:], masks[1:]):
                    value = jnp.where(mask, x[v], value)
                out[k, v] = value


def interior_kernel(flow, adj, codes, out, carry):
    sublane = lax.broadcasted_iota(jnp.int32, (8, 128), 0)
    inside = sublane < 7

    def load(i):
        rows = pl.ds(pl.multiple_of(i * 8, 8), 8)
        raw = [adj[v, rows, :] for v in range(NV)]
        code = codes[rows, :]
        state = [flow[v, rows, :] for v in range(NV)]
        return prepare(state, fluid_weight(code, raw)), raw, code, rows

    carry[...] = jnp.zeros_like(carry)

    def step(i, _):
        cell, raw, code, rows = load(i)
        acc = [carry[n] for n in range(17)]
        for axis, dim, size, mask in ((2, 1, 128, None), (1, 0, 8, inside)):
            after = moved(cell, lambda x: pltpu.roll(x, size - 1, dim))
            lower, upper = face_pair(cell, after, axis, mask)
            acc = [t + lo + pltpu.roll(hi, 1, dim) for t, lo, hi in zip(acc, lower, upper)]

        def emit(acc):
            grad = to_gradient(acc, cell)
            rho, kt, om = cell["s"][0], cell["s"][5], cell["s"][6]
            w5, w6 = BETA_STAR * cell["m"][5], BETA_OMEGA * cell["m"][6]
            grad[0] -= (w5 * kt + w6 * om) * om
            grad[5] -= w5 * rho * om
            grad[6] -= (w5 * kt + 2.0 * w6 * om) * rho
            local = jnp.where(code == 2, DAMPING, jnp.where(code == 1, 1.0, 0.0))
            for v in range(NV):
                out[v, rows, :] = grad[v] + local * raw[v]

        @pl.when(i < 7)
        def _():
            lower, upper = face_pair(cell, load(i + 1)[0], 0)
            for n in range(17):
                carry[n] = upper[n]
            emit([t + lo for t, lo in zip(acc, lower)])

        @pl.when(i == 7)
        def _():
            emit(acc)

        return 0

    lax.fori_loop(0, 8, step, 0)


def rim_kernel(plans, marks, far, grad, flow, adj, codes, *refs):
    arrays, out = refs[:-1], refs[-1]

    def ghosts(face):
        values = [far[v] for v in range(NV)] + [jnp.zeros((8, 128), jnp.float32)] * NV
        mark = marks[face]
        for at, t, steps in plans[face]:
            mask = functools.reduce(jnp.logical_or, [mark == step for step in steps])
            values = [jnp.where(mask, arrays[at][t, v], value) for v, value in enumerate(values)]
        return values

    lane = lax.broadcasted_iota(jnp.int32, (8, 128), 1)
    spans = (pl.ds(0, 8), pl.ds(56, 8), pl.ds(0, 8, stride=8), pl.ds(7, 8, stride=8))
    shares = []
    for face, rows in enumerate(spans):
        turned = marks[4 + face] == 1
        index = jnp.where(turned, 127 - lane, lane)
        values = [jnp.take_along_axis(x, index, axis=1) for x in ghosts(face)]
        swirl = jnp.where(turned, -1.0, 1.0)
        for v in (3, NV + 3):
            values[v] = values[v] * swirl
        other = prepare(values[:NV], values[NV:])
        state = [flow[v, rows, :] for v in range(NV)]
        weight = fluid_weight(codes[rows, :], [adj[v, rows, :] for v in range(NV)])
        cell = prepare(state, weight)
        if face % 2 == 0:
            acc = face_pair(other, cell, face // 2)[1]
        else:
            acc = face_pair(cell, other, face // 2)[0]
        shares.append(to_gradient(acc, cell))
    out[...] = grad[...]
    for v in range(NV):
        for rows, share in zip(spans, shares):
            out[v, rows, :] = out[v, rows, :] + share[v]

def shape(*dims, dtype=jnp.float32):
    return jax.ShapeDtypeStruct(dims, dtype)


def span(basis):
    offsets = [0]
    for b in basis:
        offsets += [o ^ b for o in offsets]
    return offsets


def solution(mesh):
    groups, peers = mesh.shape["group"], mesh.shape["block"]
    bits = peers.bit_length() - 1
    basis = [1 << i for i in range(bits - 1)] + [peers // 2]

    def within(offset):
        return [
            (g * peers + h, g * peers + (h ^ offset)) for g in range(groups) for h in range(peers)
        ]

    def between(first, offset):
        pairs = []
        for g in range(groups):
            other = (g + 1 if (g % 2 == 0) == first else g - 1) % groups
            pairs += [(g * peers + h, other * peers + (h ^ offset)) for h in range(peers)]
        return pairs

    def relay(offsets, sources, rows=2 * NV, split=False):
        arrays = []
        for x, _ in sum(sources, []):
            if not any(x is y for y in arrays):
                arrays.append(x)
        places = [[(next(n for n, y in enumerate(arrays) if y is x), k) for x, k in held] for held in sources]
        kinds, base = len(sources), len(arrays)
        if split:
            outs_of = [[(base + n * kinds + t, 0) for t in range(kinds)] for n in range(len(offsets))]
            outs = [shape(1, rows, 8, 128)] * (len(offsets) * kinds)
        else:
            outs_of = [[(base + n, t) for t in range(kinds)] for n in range(len(offsets))]
            outs = [shape(kinds, rows, 8, 128)] * len(offsets)
        return pl.pallas_call(
            functools.partial(relay_kernel, offsets, places, outs_of),
            out_shape=outs,
            in_specs=[VMEM] * base,
            out_specs=[VMEM] * len(outs),
            compiler_params=PARAMS,
            name="relay",
        )(*arrays)

    def spread(bundle, steps):
        held = {0: bundle}
        for b in steps:
            for o in list(held):
                held[o ^ b] = lax.ppermute(held[o], AXES, within(b))
        return held

    def per_device(flow_state, adjoint, cell_codes, block_links, farfield):
        links = jnp.transpose(block_links[0])
        flow, adj, codes = flow_state.reshape(NV, 64, 128), adjoint.reshape(NV, 64, 128), cell_codes.reshape(64, 128)
        hbm = [pltpu.with_memory_space_constraint(x, pltpu.HBM) for x in (links, farfield, flow_state[0], adjoint[0], cell_codes[0])]
        radial, pair, marks, outer = pl.pallas_call(
            functools.partial(pack_kernel, peers),
            out_shape=[shape(2, 2 * NV + 1, 8, 128)] * 2 + [shape(8, 8, 128, dtype=jnp.int32), shape(NV, 8, 128)],
            in_specs=[pl.BlockSpec(memory_space=pltpu.HBM)] * 5,
            out_specs=[VMEM] * 4,
            scratch_shapes=[
                pltpu.SMEM((2, 4), jnp.int32),
                pltpu.SMEM((NV,), jnp.float32),
                pltpu.VMEM((4, NV, 8, 128), jnp.float32),
                pltpu.VMEM((4, NV, 8, 128), jnp.float32),
                pltpu.VMEM((4, 8, 128), jnp.int32),
                pltpu.SemaphoreType.DMA((14,)),
            ],
            compiler_params=PARAMS,
            name="pack",
        )(*hbm)
        inner = pl.pallas_call(
            interior_kernel,
            out_shape=shape(NV, 64, 128),
            in_specs=[VMEM] * 3,
            out_specs=VMEM,
            scratch_shapes=[pltpu.VMEM((17, 8, 128), jnp.float32)],
            compiler_params=PARAMS,
            cost_estimate=pl.CostEstimate(flops=6000000, bytes_accessed=800000, transcendentals=60000),
            name="interior",
        )(flow, adj, codes)
        held_a = spread(pair, basis[-1:])
        held_r = spread(radial, basis[:-1][::-1])
        near = span(basis[:-1])[1:]
        onward = relay(near, [[(x, t) for x in held_a.values()] for t in range(2)], rows=2 * NV + 1)
        last = list(held_a.values()) + [lax.ppermute(x, AXES, within(o)) for o, x in zip(near, onward)]
        inner, last[-1] = lax.optimization_barrier((inner, last[-1]))
        choices = [[(x, t) for x in last] for t in range(2)]
        even_pair, odd_pair = relay([0], choices, split=True)
        even_pair = lax.ppermute(even_pair, AXES, between(True, 0))
        odd_pair = lax.ppermute(odd_pair, AXES, between(False, 0))
        far = span(basis[-1:])[1:]
        onward = relay(far, [[(x, t) for x in held_r.values()] for t in range(2)])
        sent = {o: lax.ppermute(x, AXES, within(o)) for o, x in zip(far, onward)}
        arrays = [even_pair, odd_pair]
        plans = [[(0, 0, [0]), (1, 0, [1])]] * 2
        for t in (1, 0):
            plan = [(x, [n]) for n, x in held_r.items() if n]
            plan += [(x, [n ^ o for n in held_r]) for o, x in sent.items()]
            plans.append([(2 + n, t, steps) for n, (_, steps) in enumerate(plan)])
        arrays += [x for x, _ in plan]
        result = pl.pallas_call(
            functools.partial(rim_kernel, plans),
            out_shape=shape(NV, 64, 128),
            in_specs=[VMEM] * (6 + len(arrays)),
            out_specs=VMEM,
            compiler_params=PARAMS,
            name="rim",
        )(marks, outer, inner, flow, adj, codes, *arrays)
        return result.reshape(flow_state.shape)

    spec = P(("group", "block"), None, None, None, None)
    return jax.shard_map(
        per_device,
        mesh=mesh,
        in_specs=(
            spec,
            spec,
            P(("group", "block"), None, None, None),
            P(("group", "block"), None, None),
            P(),
        ),
        out_specs=spec,
        check_vma=False,
    )
```

```python
import functools

import jax
import jax.numpy as jnp
from jax import lax
from jax.experimental import pallas as pl
from jax.experimental.pallas import tpu as pltpu
from jax.sharding import PartitionSpec as P

GAMMA = 1.4
MU_LAMINAR = 0.02
KAPPA_HEAT = 0.07
SIGMA_K = 0.85
SIGMA_OMEGA = 0.5
BETA_STAR = 0.09
BETA_OMEGA = 0.075
ALPHA_OMEGA = 0.52
INV_A1_SQ = 1.0 / (0.31 * 0.31)
DAMPING = 2.0

NV = 7
AXES = ("group", "block")
VMEM = pl.BlockSpec(memory_space=pltpu.VMEM)
SMEM = pl.BlockSpec(memory_space=pltpu.SMEM)
PARAMS = pltpu.CompilerParams(vmem_limit_bytes=24 << 20)


def prepare(state, weight):
    rho, u1, u2, u3, p, kt, om = state
    half_rho = 0.5 * rho
    cons = [
        rho,
        rho * u1,
        rho * u2,
        rho * u3,
        p * (1.0 / (GAMMA - 1.0)) + half_rho * (u1 * u1 + u2 * u2 + u3 * u3),
        rho * kt,
        rho * om,
    ]
    half_sound = 0.5 * jnp.sqrt(GAMMA * (p / rho))
    produce = weight[5] + (ALPHA_OMEGA * weight[6]) * (om / kt)
    return dict(s=state, m=weight, q=cons, h=half_sound, v=produce)


def moved(cell, shift):
    return dict(
        s=[shift(x) for x in cell["s"]],
        m=[shift(x) for x in cell["m"]],
        q=[shift(x) for x in cell["q"]],
        h=shift(cell["h"]),
        v=shift(cell["v"]),
    )


def sign(x):
    return jnp.where(x > 0.0, 1.0, jnp.where(x < 0.0, -1.0, 0.0))


def face_pair(low, high, axis, mask=None):
    n = 1 + axis
    sa, sc = low["s"], high["s"]
    delta = [c - a for a, c in zip(low["m"], high["m"])]
    weight_sum = low["v"] + high["v"]
    if mask is not None:
        delta = [jnp.where(mask, d, 0.0) for d in delta]
        weight_sum = jnp.where(mask, weight_sum, 0.0)
    qa = functools.reduce(jnp.add, [d * q for d, q in zip(delta, low["q"])])
    qc = functools.reduce(jnp.add, [d * q for d, q in zip(delta, high["q"])])
    half_wa, half_wc = 0.5 * sa[n], 0.5 * sc[n]
    half_lam = 0.5 * (jnp.abs(half_wa) + jnp.abs(half_wc) + low["h"] + high["h"])
    ca, cc = half_wa + half_lam, half_wc - half_lam
    slope = 0.5 * (qa - qc)

    e = [sc[i] - sa[i] for i in (1, 2, 3)]
    half_d4 = 0.5 * delta[4]
    g = [delta[i] + half_d4 * (sa[i] + sc[i]) for i in (1, 2, 3)]
    strain = e[0] * e[0] + e[1] * e[1] + e[2] * e[2]
    eg = e[0] * g[0] + e[1] * g[1] + e[2] * g[2]
    rho_m = 0.5 * (sa[0] + sc[0])
    kt_m = 0.5 * (sa[5] + sc[5])
    om_m = 0.5 * (sa[6] + sc[6])
    inv = lax.rsqrt(om_m * om_m + strain * INV_A1_SQ)
    mut = rho_m * kt_m * inv
    d_mut = (
        0.5 * (strain * weight_sum)
        - eg
        - SIGMA_K * (delta[5] * (sc[5] - sa[5]))
        - SIGMA_OMEGA * (delta[6] * (sc[6] - sa[6]))
    )
    nu = MU_LAMINAR + mut
    limited = d_mut * mut * (inv * inv)
    along = mut * weight_sum - limited * INV_A1_SQ
    k_flux = delta[5] * (MU_LAMINAR + SIGMA_K * mut)
    o_flux = delta[6] * (MU_LAMINAR + SIGMA_OMEGA * mut)
    half_inv = 0.5 * (d_mut * inv)
    k_mean = half_inv * rho_m
    rho_mean = half_inv * kt_m
    o_mean = -0.5 * (limited * om_m)
    heat = KAPPA_HEAT * delta[4]
    produced = 0.5 * (mut * strain)
    if mask is not None:
        produced = jnp.where(mask, produced, 0.0)
    side = nu * half_d4
    lower = [ca * d for d in delta]
    upper = [cc * d for d in delta]
    for i in range(3):
        jump = along * e[i] - nu * g[i]
        mean = side * e[i]
        low_u, high_u = -jump - mean, jump - mean
        if i == axis:
            low_u += 0.5 * (qa + sa[4] * delta[4]) + 0.5 * (slope * sign(sa[n]))
            high_u += 0.5 * (qc + sc[4] * delta[4]) + 0.5 * (slope * sign(sc[n]))
        lower.append(low_u)
        upper.append(high_u)
    half_dn = 0.5 * delta[n]
    lower += [half_dn + half_wa * delta[4], k_mean + k_flux, o_mean + o_flux]
    upper += [half_dn + half_wc * delta[4], k_mean - k_flux, o_mean - o_flux]
    lower += [rho_mean, heat, produced, slope]
    upper += [rho_mean, -heat, produced, slope]
    return lower, upper


def to_gradient(acc, cell):
    rho, u1, u2, u3, p, kt, om = cell["s"]
    inv_rho = 1.0 / rho
    inv_kt = 1.0 / kt
    half_wave = 0.5 * (acc[16] * cell["h"])
    heat = acc[14] * inv_rho
    y4 = acc[4]
    produced = ALPHA_OMEGA * (cell["m"][6] * acc[15]) * inv_kt
    d_rho = (
        acc[0]
        + acc[1] * u1
        + acc[2] * u2
        + acc[3] * u3
        + 0.5 * (y4 * (u1 * u1 + u2 * u2 + u3 * u3))
        + acc[5] * kt
        + acc[6] * om
        + acc[13]
        - (heat * p + half_wave) * inv_rho
    )
    return [
        d_rho,
        rho * (acc[1] + y4 * u1) + acc[7],
        rho * (acc[2] + y4 * u2) + acc[8],
        rho * (acc[3] + y4 * u3) + acc[9],
        y4 * (1.0 / (GAMMA - 1.0)) + acc[10] + heat + half_wave / p,
        rho * acc[5] + acc[11] - produced * (om * inv_kt),
        rho * acc[6] + acc[12] + produced,
    ]


def fluid_weight(code, adjoint):
    fluid = code != 1
    return [jnp.where(fluid, x, 0.0) for x in adjoint]


def pack_kernel(
    peers, links_in, farfield_in, flow_in, adj_in, codes_in, radial, pair, marks, far, links, farfield, states, weights, kinds, sems
):
    group, me = lax.axis_index("group"), lax.axis_index("block")
    copies = [pltpu.make_async_copy(links_in, links, sems.at[0]), pltpu.make_async_copy(farfield_in, farfield, sems.at[13])]
    for n, row in enumerate((0, 7)):
        copies.append(pltpu.make_async_copy(flow_in.at[:, :, row, :], states.at[n], sems.at[6 * n + 1]))
        copies.append(pltpu.make_async_copy(adj_in.at[:, :, row, :], weights.at[n], sems.at[6 * n + 2]))
        copies.append(pltpu.make_async_copy(codes_in.at[:, row, :], kinds.at[n], sems.at[6 * n + 3]))
        copies.append(pltpu.make_async_copy(flow_in.at[:, row], states.at[2 + n], sems.at[6 * n + 4]))
        copies.append(pltpu.make_async_copy(adj_in.at[:, row], weights.at[2 + n], sems.at[6 * n + 5]))
        copies.append(pltpu.make_async_copy(codes_in.at[row], kinds.at[2 + n], sems.at[6 * n + 6]))
    for copy in copies:
        copy.start()
    for copy in copies:
        copy.wait()

    upper_half = lax.broadcasted_iota(jnp.int32, (8, 128), 0) >= 4

    def layers(out, faces):
        goals = []
        for t, (n, partner) in enumerate(faces):
            fluid = kinds[n] != 1
            for v in range(NV):
                out[2 * NV * t + v] = states[n, v]
                out[2 * NV * t + NV + v] = jnp.where(fluid, weights[n, v], 0.0)
            goals.append(jnp.where(partner >= 0, lax.rem(partner, peers), -1).astype(jnp.float32))
        out[4 * NV] = jnp.where(upper_half, goals[1], goals[0])

    layers(radial, [(0, links[0, 2]), (1, links[0, 3])])
    even = lax.rem(group, 2) == 0
    forward, backward = (3, links[0, 1]), (2, links[0, 0])
    layers(
        pair,
        [
            [jnp.where(flag, x, y) for x, y in zip(forward, backward)]
            for flag in (even, jnp.logical_not(even))
        ],
    )
    for face in range(4):
        partner = links[0, face]
        if face < 2:
            source = jnp.where(even, 1 - face, face)
        else:
            source = lax.rem(jnp.maximum(partner, 0), peers) ^ me
        marks[face] = jnp.full((8, 128), jnp.where(partner >= 0, source, -1))
        marks[4 + face] = jnp.full((8, 128), links[1, face])
    for v in range(NV):
        far[v] = jnp.full((8, 128), farfield[v])


def relay_kernel(offsets, sources, outs_of, *refs):
    me = lax.axis_index("block")
    upper_half = lax.broadcasted_iota(jnp.int32, (8, 128), 0) >= 4
    kept = [[] for _ in offsets]
    for t, places in enumerate(sources):
        goals = [jnp.broadcast_to(refs[at][4 * NV, 4 * k : 4 * k + 1, :], (8, 128)) for at, k in places]
        for n, (offset, outs) in enumerate(zip(offsets, outs_of)):
            wanted = (me ^ offset).astype(jnp.float32)
            masks = [goal == wanted for goal in goals]
            found = functools.reduce(jnp.logical_or, masks)
            kept[n].append(jnp.where(found, wanted, -1.0))
            to, place = outs[t]
            for v in range(2 * NV):
                value, *others = [refs[at][2 * NV * k + v] for at, k in places]
                for x, mask in zip(others, masks[1:]):
                    value = jnp.where(mask, x, value)
                refs[to][2 * NV * place + v] = value
    for goals, outs in zip(kept, outs_of):
        if refs[outs[0][0]].shape[0] > 4 * NV:
            refs[outs[0][0]][4 * NV] = jnp.where(upper_half, goals[1], goals[0])


def interior_kernel(flow, adj, codes, out, carry):
    sublane = lax.broadcasted_iota(jnp.int32, (8, 128), 0)
    inside = sublane < 7

    def load(i):
        rows = pl.ds(pl.multiple_of(i * 8, 8), 8)
        raw = [adj[v, rows, :] for v in range(NV)]
        code = codes[rows, :]
        state = [flow[v, rows, :] for v in range(NV)]
        return prepare(state, fluid_weight(code, raw)), raw, code, rows

    carry[...] = jnp.zeros_like(carry)

    def step(i, _):
        cell, raw, code, rows = load(i)
        acc = [carry[n] for n in range(17)]
        for axis, dim, size, mask in ((2, 1, 128, None), (1, 0, 8, inside)):
            after = moved(cell, lambda x: pltpu.roll(x, size - 1, dim))
            lower, upper = face_pair(cell, after, axis, mask)
            acc = [t + lo + pltpu.roll(hi, 1, dim) for t, lo, hi in zip(acc, lower, upper)]

        def emit(acc):
            grad = to_gradient(acc, cell)
            rho, kt, om = cell["s"][0], cell["s"][5], cell["s"][6]
            w5, w6 = BETA_STAR * cell["m"][5], BETA_OMEGA * cell["m"][6]
            grad[0] -= (w5 * kt + w6 * om) * om
            grad[5] -= w5 * rho * om
            grad[6] -= (w5 * kt + 2.0 * w6 * om) * rho
            local = jnp.where(code == 2, DAMPING, jnp.where(code == 1, 1.0, 0.0))
            for v in range(NV):
                out[v, rows, :] = grad[v] + local * raw[v]

        @pl.when(i < 7)
        def _():
            lower, upper = face_pair(cell, load(i + 1)[0], 0)
            for n in range(17):
                carry[n] = upper[n]
            emit([t + lo for t, lo in zip(acc, lower)])

        @pl.when(i == 7)
        def _():
            emit(acc)

        return 0

    lax.fori_loop(0, 8, step, 0)


def rim_kernel(plans, marks, far, grad, flow, adj, codes, *refs):
    arrays, out = refs[:-1], refs[-1]

    def ghosts(face):
        values = [far[v] for v in range(NV)] + [jnp.zeros((8, 128), jnp.float32)] * NV
        mark = marks[face]
        for at, t, steps in plans[face]:
            mask = functools.reduce(jnp.logical_or, [mark == step for step in steps])
            values = [jnp.where(mask, arrays[at][2 * NV * t + v], value) for v, value in enumerate(values)]
        return values

    lane = lax.broadcasted_iota(jnp.int32, (8, 128), 1)
    spans = (pl.ds(0, 8), pl.ds(56, 8), pl.ds(0, 8, stride=8), pl.ds(7, 8, stride=8))
    shares = []
    for face, rows in enumerate(spans):
        turned = marks[4 + face] == 1
        index = jnp.where(turned, 127 - lane, lane)
        values = [jnp.take_along_axis(x, index, axis=1) for x in ghosts(face)]
        swirl = jnp.where(turned, -1.0, 1.0)
        for v in (3, NV + 3):
            values[v] = values[v] * swirl
        other = prepare(values[:NV], values[NV:])
        state = [flow[v, rows, :] for v in range(NV)]
        weight = fluid_weight(codes[rows, :], [adj[v, rows, :] for v in range(NV)])
        cell = prepare(state, weight)
        if face % 2 == 0:
            acc = face_pair(other, cell, face // 2)[1]
        else:
            acc = face_pair(cell, other, face // 2)[0]
        shares.append(to_gradient(acc, cell))
    out[...] = grad[...]
    for v in range(NV):
        for rows, share in zip(spans, shares):
            out[v, rows, :] = out[v, rows, :] + share[v]

def shape(*dims, dtype=jnp.float32):
    return jax.ShapeDtypeStruct(dims, dtype)


def span(basis):
    offsets = [0]
    for b in basis:
        offsets += [o ^ b for o in offsets]
    return offsets


def solution(mesh):
    groups, peers = mesh.shape["group"], mesh.shape["block"]
    bits = peers.bit_length() - 1
    basis = [1 << i for i in range(bits - 1)] + [peers // 2]

    def within(offset):
        return [
            (g * peers + h, g * peers + (h ^ offset)) for g in range(groups) for h in range(peers)
        ]

    def between(first, offset):
        pairs = []
        for g in range(groups):
            other = (g + 1 if (g % 2 == 0) == first else g - 1) % groups
            pairs += [(g * peers + h, other * peers + (h ^ offset)) for h in range(peers)]
        return pairs

    def relay(offsets, sources, rows=4 * NV, split=False):
        arrays = []
        for x, _ in sum(sources, []):
            if not any(x is y for y in arrays):
                arrays.append(x)
        places = [[(next(n for n, y in enumerate(arrays) if y is x), k) for x, k in held] for held in sources]
        kinds, base = len(sources), len(arrays)
        if split:
            outs_of = [[(base + n * kinds + t, 0) for t in range(kinds)] for n in range(len(offsets))]
            outs = [shape(2 * NV, 8, 128)] * (len(offsets) * kinds)
        else:
            outs_of = [[(base + n, t) for t in range(kinds)] for n in range(len(offsets))]
            outs = [shape(rows, 8, 128)] * len(offsets)
        return pl.pallas_call(
            functools.partial(relay_kernel, offsets, places, outs_of),
            out_shape=outs,
            in_specs=[VMEM] * base,
            out_specs=[VMEM] * len(outs),
            compiler_params=PARAMS,
            name="relay",
        )(*arrays)

    def spread(bundle, steps):
        held = {0: bundle}
        for b in steps:
            for o in list(held):
                held[o ^ b] = lax.ppermute(held[o], AXES, within(b))
        return held

    def per_device(flow_state, adjoint, cell_codes, block_links, farfield):
        links = jnp.transpose(block_links[0])
        flow, adj, codes = flow_state.reshape(NV, 64, 128), adjoint.reshape(NV, 64, 128), cell_codes.reshape(64, 128)
        hbm = [pltpu.with_memory_space_constraint(x, pltpu.HBM) for x in (links, farfield, flow_state[0], adjoint[0], cell_codes[0])]
        radial, pair, marks, outer = pl.pallas_call(
            functools.partial(pack_kernel, peers),
            out_shape=[shape(4 * NV + 1, 8, 128)] * 2 + [shape(8, 8, 128, dtype=jnp.int32), shape(NV, 8, 128)],
            in_specs=[pl.BlockSpec(memory_space=pltpu.HBM)] * 5,
            out_specs=[VMEM] * 4,
            scratch_shapes=[
                pltpu.SMEM((2, 4), jnp.int32),
                pltpu.SMEM((NV,), jnp.float32),
                pltpu.VMEM((4, NV, 8, 128), jnp.float32),
                pltpu.VMEM((4, NV, 8, 128), jnp.float32),
                pltpu.VMEM((4, 8, 128), jnp.int32),
                pltpu.SemaphoreType.DMA((14,)),
            ],
            compiler_params=PARAMS,
            name="pack",
        )(*hbm)
        held_r = spread(radial, basis[:-1][::-1])
        held_a = spread(pair, basis[-1:])
        near = sorted(span(basis[:-1])[1:], key=lambda o: (not o & 1, o))
        onward = relay(near, [[(x, t) for x in held_a.values()] for t in range(2)], rows=4 * NV + 1)
        last = list(held_a.values()) + [lax.ppermute(x, AXES, within(o)) for o, x in zip(near, onward)]
        choices = [[(x, t) for x in last] for t in range(2)]
        even_pair, odd_pair = relay([0], choices, split=True)
        even_pair, odd_pair, flow, adj, codes = lax.optimization_barrier((even_pair, odd_pair, flow, adj, codes))
        even_pair = lax.ppermute(even_pair, AXES, between(True, 0))
        odd_pair = lax.ppermute(odd_pair, AXES, between(False, 0))
        far = span(basis[-1:])[1:]
        onward = relay(far, [[(x, t) for x in held_r.values()] for t in range(2)])
        sent = {o: lax.ppermute(x, AXES, within(o)) for o, x in zip(far, onward)}
        inner = pl.pallas_call(
            interior_kernel,
            out_shape=shape(NV, 64, 128),
            in_specs=[VMEM] * 3,
            out_specs=VMEM,
            scratch_shapes=[pltpu.VMEM((17, 8, 128), jnp.float32)],
            compiler_params=PARAMS,
            cost_estimate=pl.CostEstimate(flops=6000000, bytes_accessed=800000, transcendentals=60000),
            name="interior",
        )(flow, adj, codes)
        arrays = [even_pair, odd_pair]
        plans = [[(0, 0, [0]), (1, 0, [1])]] * 2
        for t in (1, 0):
            plan = [(x, [n]) for n, x in held_r.items() if n]
            plan += [(x, [n ^ o for n in held_r]) for o, x in sent.items()]
            plans.append([(2 + n, t, steps) for n, (_, steps) in enumerate(plan)])
        arrays += [x for x, _ in plan]
        result = pl.pallas_call(
            functools.partial(rim_kernel, plans),
            out_shape=shape(NV, 64, 128),
            in_specs=[VMEM] * (6 + len(arrays)),
            out_specs=VMEM,
            compiler_params=PARAMS,
            name="rim",
        )(marks, outer, inner, flow, adj, codes, *arrays)
        return result.reshape(flow_state.shape)

    spec = P(("group", "block"), None, None, None, None)
    return jax.shard_map(
        per_device,
        mesh=mesh,
        in_specs=(
            spec,
            spec,
            P(("group", "block"), None, None, None),
            P(("group", "block"), None, None),
            P(),
        ),
        out_specs=spec,
        check_vma=False,
    )
```

```python
import functools

import jax
import jax.numpy as jnp
from jax import lax
from jax.experimental import pallas as pl
from jax.experimental.pallas import tpu as pltpu
from jax.sharding import PartitionSpec as P

GAMMA = 1.4
MU_LAMINAR = 0.02
KAPPA_HEAT = 0.07
SIGMA_K = 0.85
SIGMA_OMEGA = 0.5
BETA_STAR = 0.09
BETA_OMEGA = 0.075
ALPHA_OMEGA = 0.52
INV_A1_SQ = 1.0 / (0.31 * 0.31)
DAMPING = 2.0

NV = 7
AXES = ("group", "block")
VMEM = pl.BlockSpec(memory_space=pltpu.VMEM)
SMEM = pl.BlockSpec(memory_space=pltpu.SMEM)
PARAMS = pltpu.CompilerParams(vmem_limit_bytes=24 << 20)


def prepare(state, weight):
    rho, u1, u2, u3, p, kt, om = state
    half_rho = 0.5 * rho
    cons = [
        rho,
        rho * u1,
        rho * u2,
        rho * u3,
        p * (1.0 / (GAMMA - 1.0)) + half_rho * (u1 * u1 + u2 * u2 + u3 * u3),
        rho * kt,
        rho * om,
    ]
    half_sound = 0.5 * jnp.sqrt(GAMMA * (p / rho))
    produce = weight[5] + (ALPHA_OMEGA * weight[6]) * (om / kt)
    return dict(s=state, m=weight, q=cons, h=half_sound, v=produce)


def moved(cell, shift):
    return dict(
        s=[shift(x) for x in cell["s"]],
        m=[shift(x) for x in cell["m"]],
        q=[shift(x) for x in cell["q"]],
        h=shift(cell["h"]),
        v=shift(cell["v"]),
    )


def sign(x):
    return jnp.where(x > 0.0, 1.0, jnp.where(x < 0.0, -1.0, 0.0))


def face_pair(low, high, axis, mask=None):
    n = 1 + axis
    sa, sc = low["s"], high["s"]
    delta = [c - a for a, c in zip(low["m"], high["m"])]
    weight_sum = low["v"] + high["v"]
    if mask is not None:
        delta = [jnp.where(mask, d, 0.0) for d in delta]
        weight_sum = jnp.where(mask, weight_sum, 0.0)
    qa = functools.reduce(jnp.add, [d * q for d, q in zip(delta, low["q"])])
    qc = functools.reduce(jnp.add, [d * q for d, q in zip(delta, high["q"])])
    half_wa, half_wc = 0.5 * sa[n], 0.5 * sc[n]
    half_lam = 0.5 * (jnp.abs(half_wa) + jnp.abs(half_wc) + low["h"] + high["h"])
    ca, cc = half_wa + half_lam, half_wc - half_lam
    slope = 0.5 * (qa - qc)

    e = [sc[i] - sa[i] for i in (1, 2, 3)]
    half_d4 = 0.5 * delta[4]
    g = [delta[i] + half_d4 * (sa[i] + sc[i]) for i in (1, 2, 3)]
    strain = e[0] * e[0] + e[1] * e[1] + e[2] * e[2]
    eg = e[0] * g[0] + e[1] * g[1] + e[2] * g[2]
    rho_m = 0.5 * (sa[0] + sc[0])
    kt_m = 0.5 * (sa[5] + sc[5])
    om_m = 0.5 * (sa[6] + sc[6])
    inv = lax.rsqrt(om_m * om_m + strain * INV_A1_SQ)
    mut = rho_m * kt_m * inv
    d_mut = (
        0.5 * (strain * weight_sum)
        - eg
        - SIGMA_K * (delta[5] * (sc[5] - sa[5]))
        - SIGMA_OMEGA * (delta[6] * (sc[6] - sa[6]))
    )
    nu = MU_LAMINAR + mut
    limited = d_mut * mut * (inv * inv)
    along = mut * weight_sum - limited * INV_A1_SQ
    k_flux = delta[5] * (MU_LAMINAR + SIGMA_K * mut)
    o_flux = delta[6] * (MU_LAMINAR + SIGMA_OMEGA * mut)
    half_inv = 0.5 * (d_mut * inv)
    k_mean = half_inv * rho_m
    rho_mean = half_inv * kt_m
    o_mean = -0.5 * (limited * om_m)
    heat = KAPPA_HEAT * delta[4]
    produced = 0.5 * (mut * strain)
    if mask is not None:
        produced = jnp.where(mask, produced, 0.0)
    side = nu * half_d4
    lower = [ca * d for d in delta]
    upper = [cc * d for d in delta]
    for i in range(3):
        jump = along * e[i] - nu * g[i]
        mean = side * e[i]
        low_u, high_u = -jump - mean, jump - mean
        if i == axis:
            low_u += 0.5 * (qa + sa[4] * delta[4]) + 0.5 * (slope * sign(sa[n]))
            high_u += 0.5 * (qc + sc[4] * delta[4]) + 0.5 * (slope * sign(sc[n]))
        lower.append(low_u)
        upper.append(high_u)
    half_dn = 0.5 * delta[n]
    lower += [half_dn + half_wa * delta[4], k_mean + k_flux, o_mean + o_flux]
    upper += [half_dn + half_wc * delta[4], k_mean - k_flux, o_mean - o_flux]
    lower += [rho_mean, heat, produced, slope]
    upper += [rho_mean, -heat, produced, slope]
    return lower, upper


def to_gradient(acc, cell):
    rho, u1, u2, u3, p, kt, om = cell["s"]
    inv_rho = 1.0 / rho
    inv_kt = 1.0 / kt
    half_wave = 0.5 * (acc[16] * cell["h"])
    heat = acc[14] * inv_rho
    y4 = acc[4]
    produced = ALPHA_OMEGA * (cell["m"][6] * acc[15]) * inv_kt
    d_rho = (
        acc[0]
        + acc[1] * u1
        + acc[2] * u2
        + acc[3] * u3
        + 0.5 * (y4 * (u1 * u1 + u2 * u2 + u3 * u3))
        + acc[5] * kt
        + acc[6] * om
        + acc[13]
        - (heat * p + half_wave) * inv_rho
    )
    return [
        d_rho,
        rho * (acc[1] + y4 * u1) + acc[7],
        rho * (acc[2] + y4 * u2) + acc[8],
        rho * (acc[3] + y4 * u3) + acc[9],
        y4 * (1.0 / (GAMMA - 1.0)) + acc[10] + heat + half_wave / p,
        rho * acc[5] + acc[11] - produced * (om * inv_kt),
        rho * acc[6] + acc[12] + produced,
    ]


def fluid_weight(code, adjoint):
    fluid = code != 1
    return [jnp.where(fluid, x, 0.0) for x in adjoint]


def pack_kernel(
    peers, links_in, farfield_in, flow_in, adj_in, codes_in, radial, pair, marks, far, links, farfield, states, weights, kinds, sems
):
    group, me = lax.axis_index("group"), lax.axis_index("block")
    copies = [pltpu.make_async_copy(links_in, links, sems.at[0]), pltpu.make_async_copy(farfield_in, farfield, sems.at[13])]
    for n, row in enumerate((0, 7)):
        copies.append(pltpu.make_async_copy(flow_in.at[:, :, row, :], states.at[n], sems.at[6 * n + 1]))
        copies.append(pltpu.make_async_copy(adj_in.at[:, :, row, :], weights.at[n], sems.at[6 * n + 2]))
        copies.append(pltpu.make_async_copy(codes_in.at[:, row, :], kinds.at[n], sems.at[6 * n + 3]))
        copies.append(pltpu.make_async_copy(flow_in.at[:, row], states.at[2 + n], sems.at[6 * n + 4]))
        copies.append(pltpu.make_async_copy(adj_in.at[:, row], weights.at[2 + n], sems.at[6 * n + 5]))
        copies.append(pltpu.make_async_copy(codes_in.at[row], kinds.at[2 + n], sems.at[6 * n + 6]))
    for copy in copies:
        copy.start()
    for copy in copies:
        copy.wait()

    upper_half = lax.broadcasted_iota(jnp.int32, (8, 128), 0) >= 4

    def layers(out, faces):
        goals = []
        for t, (n, partner) in enumerate(faces):
            fluid = kinds[n] != 1
            for v in range(NV):
                out[2 * NV * t + v] = states[n, v]
                out[2 * NV * t + NV + v] = jnp.where(fluid, weights[n, v], 0.0)
            goals.append(jnp.where(partner >= 0, lax.rem(partner, peers), -1).astype(jnp.float32))
        out[4 * NV] = jnp.where(upper_half, goals[1], goals[0])

    layers(radial, [(0, links[0, 2]), (1, links[0, 3])])
    even = lax.rem(group, 2) == 0
    forward, backward = (3, links[0, 1]), (2, links[0, 0])
    layers(
        pair,
        [
            [jnp.where(flag, x, y) for x, y in zip(forward, backward)]
            for flag in (even, jnp.logical_not(even))
        ],
    )
    for face in range(4):
        partner = links[0, face]
        if face < 2:
            source = jnp.where(even, 1 - face, face)
        else:
            source = lax.rem(jnp.maximum(partner, 0), peers) ^ me
        marks[face] = jnp.full((8, 128), jnp.where(partner >= 0, source, -1))
        marks[4 + face] = jnp.full((8, 128), links[1, face])
    for v in range(NV):
        far[v] = jnp.full((8, 128), farfield[v])


def relay_kernel(offsets, sources, outs_of, *refs):
    me = lax.axis_index("block")
    upper_half = lax.broadcasted_iota(jnp.int32, (8, 128), 0) >= 4
    kept = [[] for _ in offsets]
    for t, places in enumerate(sources):
        goals = [jnp.broadcast_to(refs[at][4 * NV, 4 * k : 4 * k + 1, :], (8, 128)) for at, k in places]
        for n, (offset, outs) in enumerate(zip(offsets, outs_of)):
            wanted = (me ^ offset).astype(jnp.float32)
            masks = [goal == wanted for goal in goals]
            found = functools.reduce(jnp.logical_or, masks)
            kept[n].append(jnp.where(found, wanted, -1.0))
            to, place = outs[t]
            for v in range(2 * NV):
                value, *others = [refs[at][2 * NV * k + v] for at, k in places]
                for x, mask in zip(others, masks[1:]):
                    value = jnp.where(mask, x, value)
                refs[to][2 * NV * place + v] = value
    for goals, outs in zip(kept, outs_of):
        if refs[outs[0][0]].shape[0] > 4 * NV:
            refs[outs[0][0]][4 * NV] = jnp.where(upper_half, goals[1], goals[0])


def interior_kernel(flow, adj, codes, out, carry):
    sublane = lax.broadcasted_iota(jnp.int32, (8, 128), 0)
    inside = sublane < 7

    def load(i):
        rows = pl.ds(pl.multiple_of(i * 8, 8), 8)
        raw = [adj[v, rows, :] for v in range(NV)]
        code = codes[rows, :]
        state = [flow[v, rows, :] for v in range(NV)]
        return prepare(state, fluid_weight(code, raw)), raw, code, rows

    carry[...] = jnp.zeros_like(carry)

    def step(i, _):
        cell, raw, code, rows = load(i)
        acc = [carry[n] for n in range(17)]
        for axis, dim, size, mask in ((2, 1, 128, None), (1, 0, 8, inside)):
            after = moved(cell, lambda x: pltpu.roll(x, size - 1, dim))
            lower, upper = face_pair(cell, after, axis, mask)
            acc = [t + lo + pltpu.roll(hi, 1, dim) for t, lo, hi in zip(acc, lower, upper)]

        def emit(acc):
            grad = to_gradient(acc, cell)
            rho, kt, om = cell["s"][0], cell["s"][5], cell["s"][6]
            w5, w6 = BETA_STAR * cell["m"][5], BETA_OMEGA * cell["m"][6]
            grad[0] -= (w5 * kt + w6 * om) * om
            grad[5] -= w5 * rho * om
            grad[6] -= (w5 * kt + 2.0 * w6 * om) * rho
            local = jnp.where(code == 2, DAMPING, jnp.where(code == 1, 1.0, 0.0))
            for v in range(NV):
                out[v, rows, :] = grad[v] + local * raw[v]

        @pl.when(i < 7)
        def _():
            lower, upper = face_pair(cell, load(i + 1)[0], 0)
            for n in range(17):
                carry[n] = upper[n]
            emit([t + lo for t, lo in zip(acc, lower)])

        @pl.when(i == 7)
        def _():
            emit(acc)

        return 0

    lax.fori_loop(0, 8, step, 0)


def rim_kernel(faces, plans, marks, far, grad, flow, adj, codes, *refs):
    arrays, out = refs[:-1], refs[-1]

    def ghosts(face):
        values = [far[v] for v in range(NV)] + [jnp.zeros((8, 128), jnp.float32)] * NV
        mark = marks[face]
        for at, t, steps in plans[face]:
            mask = functools.reduce(jnp.logical_or, [mark == step for step in steps])
            values = [jnp.where(mask, arrays[at][2 * NV * t + v], value) for v, value in enumerate(values)]
        return values

    lane = lax.broadcasted_iota(jnp.int32, (8, 128), 1)
    spans = (pl.ds(0, 8), pl.ds(56, 8), pl.ds(0, 8, stride=8), pl.ds(7, 8, stride=8))
    shares = []
    for face in faces:
        rows = spans[face]
        turned = marks[4 + face] == 1
        index = jnp.where(turned, 127 - lane, lane)
        values = [jnp.take_along_axis(x, index, axis=1) for x in ghosts(face)]
        swirl = jnp.where(turned, -1.0, 1.0)
        for v in (3, NV + 3):
            values[v] = values[v] * swirl
        other = prepare(values[:NV], values[NV:])
        state = [flow[v, rows, :] for v in range(NV)]
        weight = fluid_weight(codes[rows, :], [adj[v, rows, :] for v in range(NV)])
        cell = prepare(state, weight)
        if face % 2 == 0:
            acc = face_pair(other, cell, face // 2)[1]
        else:
            acc = face_pair(cell, other, face // 2)[0]
        shares.append(to_gradient(acc, cell))
    out[...] = grad[...]
    for v in range(NV):
        for rows, share in zip([spans[f] for f in faces], shares):
            out[v, rows, :] = out[v, rows, :] + share[v]

def shape(*dims, dtype=jnp.float32):
    return jax.ShapeDtypeStruct(dims, dtype)


def span(basis):
    offsets = [0]
    for b in basis:
        offsets += [o ^ b for o in offsets]
    return offsets


def solution(mesh):
    groups, peers = mesh.shape["group"], mesh.shape["block"]
    bits = peers.bit_length() - 1
    basis = [1 << i for i in range(bits - 1)] + [peers // 2]

    def within(offset):
        return [
            (g * peers + h, g * peers + (h ^ offset)) for g in range(groups) for h in range(peers)
        ]

    def between(first, offset):
        pairs = []
        for g in range(groups):
            other = (g + 1 if (g % 2 == 0) == first else g - 1) % groups
            pairs += [(g * peers + h, other * peers + (h ^ offset)) for h in range(peers)]
        return pairs

    def relay(offsets, sources, rows=4 * NV, split=False):
        arrays = []
        for x, _ in sum(sources, []):
            if not any(x is y for y in arrays):
                arrays.append(x)
        places = [[(next(n for n, y in enumerate(arrays) if y is x), k) for x, k in held] for held in sources]
        kinds, base = len(sources), len(arrays)
        if split:
            outs_of = [[(base + n * kinds + t, 0) for t in range(kinds)] for n in range(len(offsets))]
            outs = [shape(2 * NV, 8, 128)] * (len(offsets) * kinds)
        else:
            outs_of = [[(base + n, t) for t in range(kinds)] for n in range(len(offsets))]
            outs = [shape(rows, 8, 128)] * len(offsets)
        return pl.pallas_call(
            functools.partial(relay_kernel, offsets, places, outs_of),
            out_shape=outs,
            in_specs=[VMEM] * base,
            out_specs=[VMEM] * len(outs),
            compiler_params=PARAMS,
            name="relay",
        )(*arrays)

    def spread(bundle, steps):
        held = {0: bundle}
        for b in steps:
            for o in list(held):
                held[o ^ b] = lax.ppermute(held[o], AXES, within(b))
        return held

    def per_device(flow_state, adjoint, cell_codes, block_links, farfield):
        links = jnp.transpose(block_links[0])
        flow, adj, codes = flow_state.reshape(NV, 64, 128), adjoint.reshape(NV, 64, 128), cell_codes.reshape(64, 128)
        hbm = [pltpu.with_memory_space_constraint(x, pltpu.HBM) for x in (links, farfield, flow_state[0], adjoint[0], cell_codes[0])]
        radial, pair, marks, outer = pl.pallas_call(
            functools.partial(pack_kernel, peers),
            out_shape=[shape(4 * NV + 1, 8, 128)] * 2 + [shape(8, 8, 128, dtype=jnp.int32), shape(NV, 8, 128)],
            in_specs=[pl.BlockSpec(memory_space=pltpu.HBM)] * 5,
            out_specs=[VMEM] * 4,
            scratch_shapes=[
                pltpu.SMEM((2, 4), jnp.int32),
                pltpu.SMEM((NV,), jnp.float32),
                pltpu.VMEM((4, NV, 8, 128), jnp.float32),
                pltpu.VMEM((4, NV, 8, 128), jnp.float32),
                pltpu.VMEM((4, 8, 128), jnp.int32),
                pltpu.SemaphoreType.DMA((14,)),
            ],
            compiler_params=PARAMS,
            name="pack",
        )(*hbm)
        held_r = spread(radial, basis[:-1][::-1])
        held_a = spread(pair, basis[-1:])
        near = sorted(span(basis[:-1])[1:], key=lambda o: (not o & 1, o))
        onward = relay(near, [[(x, t) for x in held_a.values()] for t in range(2)], rows=4 * NV + 1)
        last = list(held_a.values()) + [lax.ppermute(x, AXES, within(o)) for o, x in zip(near, onward)]
        inner = pl.pallas_call(
            interior_kernel,
            out_shape=shape(NV, 64, 128),
            in_specs=[VMEM] * 3,
            out_specs=VMEM,
            scratch_shapes=[pltpu.VMEM((17, 8, 128), jnp.float32)],
            compiler_params=PARAMS,
            cost_estimate=pl.CostEstimate(flops=6000000, bytes_accessed=800000, transcendentals=60000),
            name="interior",
        )(flow, adj, codes)
        first = len(held_a)
        inner, last[first] = lax.optimization_barrier((inner, last[first]))
        choices = [[(x, t) for x in last] for t in range(2)]
        even_pair, odd_pair = relay([0], choices, split=True)
        even_pair = lax.ppermute(even_pair, AXES, between(True, 0))
        odd_pair = lax.ppermute(odd_pair, AXES, between(False, 0))
        far = span(basis[-1:])[1:]
        onward = relay(far, [[(x, t) for x in held_r.values()] for t in range(2)])
        sent = {o: lax.ppermute(x, AXES, within(o)) for o, x in zip(far, onward)}
        axial_plan = [(0, 0, [0]), (1, 0, [1])]
        plan = [(x, [n]) for n, x in held_r.items() if n]
        plan += [(x, [n ^ o for n in held_r]) for o, x in sent.items()]
        low, high = [[(n, t, steps) for n, (_, steps) in enumerate(plan)] for t in range(2)]
        plans = [axial_plan, axial_plan, high, low]
        result = inner
        for faces, arrays in (((2, 3), [x for x, _ in plan]), ((0, 1), [even_pair, odd_pair])):
            result = pl.pallas_call(
                functools.partial(rim_kernel, faces, plans),
                out_shape=shape(NV, 64, 128),
                in_specs=[VMEM] * (6 + len(arrays)),
                out_specs=VMEM,
                compiler_params=PARAMS,
                cost_estimate=pl.CostEstimate(flops=1000000, bytes_accessed=900000, transcendentals=20000),
                name="rim",
            )(marks, outer, result, flow, adj, codes, *arrays)
        return result.reshape(flow_state.shape)

    spec = P(("group", "block"), None, None, None, None)
    return jax.shard_map(
        per_device,
        mesh=mesh,
        in_specs=(
            spec,
            spec,
            P(("group", "block"), None, None, None),
            P(("group", "block"), None, None),
            P(),
        ),
        out_specs=spec,
        check_vma=False,
    )
```

```python
import functools

import jax
import jax.numpy as jnp
from jax import lax
from jax.experimental import pallas as pl
from jax.experimental.pallas import tpu as pltpu
from jax.sharding import PartitionSpec as P

GAMMA = 1.4
MU_LAMINAR = 0.02
KAPPA_HEAT = 0.07
SIGMA_K = 0.85
SIGMA_OMEGA = 0.5
BETA_STAR = 0.09
BETA_OMEGA = 0.075
ALPHA_OMEGA = 0.52
INV_A1_SQ = 1.0 / (0.31 * 0.31)
DAMPING = 2.0

NV = 7
AXES = ("group", "block")
VMEM = pl.BlockSpec(memory_space=pltpu.VMEM)
SMEM = pl.BlockSpec(memory_space=pltpu.SMEM)
PARAMS = pltpu.CompilerParams(vmem_limit_bytes=24 << 20)


def prepare(state, weight):
    rho, u1, u2, u3, p, kt, om = state
    half_rho = 0.5 * rho
    cons = [
        rho,
        rho * u1,
        rho * u2,
        rho * u3,
        p * (1.0 / (GAMMA - 1.0)) + half_rho * (u1 * u1 + u2 * u2 + u3 * u3),
        rho * kt,
        rho * om,
    ]
    half_sound = 0.5 * jnp.sqrt(GAMMA * (p / rho))
    produce = weight[5] + (ALPHA_OMEGA * weight[6]) * (om / kt)
    return dict(s=state, m=weight, q=cons, h=half_sound, v=produce)


def moved(cell, shift):
    return dict(
        s=[shift(x) for x in cell["s"]],
        m=[shift(x) for x in cell["m"]],
        q=[shift(x) for x in cell["q"]],
        h=shift(cell["h"]),
        v=shift(cell["v"]),
    )


def sign(x):
    return jnp.where(x > 0.0, 1.0, jnp.where(x < 0.0, -1.0, 0.0))


def face_pair(low, high, axis, mask=None):
    n = 1 + axis
    sa, sc = low["s"], high["s"]
    delta = [c - a for a, c in zip(low["m"], high["m"])]
    weight_sum = low["v"] + high["v"]
    if mask is not None:
        delta = [jnp.where(mask, d, 0.0) for d in delta]
        weight_sum = jnp.where(mask, weight_sum, 0.0)
    qa = functools.reduce(jnp.add, [d * q for d, q in zip(delta, low["q"])])
    qc = functools.reduce(jnp.add, [d * q for d, q in zip(delta, high["q"])])
    half_wa, half_wc = 0.5 * sa[n], 0.5 * sc[n]
    half_lam = 0.5 * (jnp.abs(half_wa) + jnp.abs(half_wc) + low["h"] + high["h"])
    ca, cc = half_wa + half_lam, half_wc - half_lam
    slope = 0.5 * (qa - qc)

    e = [sc[i] - sa[i] for i in (1, 2, 3)]
    half_d4 = 0.5 * delta[4]
    g = [delta[i] + half_d4 * (sa[i] + sc[i]) for i in (1, 2, 3)]
    strain = e[0] * e[0] + e[1] * e[1] + e[2] * e[2]
    eg = e[0] * g[0] + e[1] * g[1] + e[2] * g[2]
    rho_m = 0.5 * (sa[0] + sc[0])
    kt_m = 0.5 * (sa[5] + sc[5])
    om_m = 0.5 * (sa[6] + sc[6])
    inv = lax.rsqrt(om_m * om_m + strain * INV_A1_SQ)
    mut = rho_m * kt_m * inv
    d_mut = (
        0.5 * (strain * weight_sum)
        - eg
        - SIGMA_K * (delta[5] * (sc[5] - sa[5]))
        - SIGMA_OMEGA * (delta[6] * (sc[6] - sa[6]))
    )
    nu = MU_LAMINAR + mut
    limited = d_mut * mut * (inv * inv)
    along = mut * weight_sum - limited * INV_A1_SQ
    k_flux = delta[5] * (MU_LAMINAR + SIGMA_K * mut)
    o_flux = delta[6] * (MU_LAMINAR + SIGMA_OMEGA * mut)
    half_inv = 0.5 * (d_mut * inv)
    k_mean = half_inv * rho_m
    rho_mean = half_inv * kt_m
    o_mean = -0.5 * (limited * om_m)
    heat = KAPPA_HEAT * delta[4]
    produced = 0.5 * (mut * strain)
    if mask is not None:
        produced = jnp.where(mask, produced, 0.0)
    side = nu * half_d4
    lower = [ca * d for d in delta]
    upper = [cc * d for d in delta]
    for i in range(3):
        jump = along * e[i] - nu * g[i]
        mean = side * e[i]
        low_u, high_u = -jump - mean, jump - mean
        if i == axis:
            low_u += 0.5 * (qa + sa[4] * delta[4]) + 0.5 * (slope * sign(sa[n]))
            high_u += 0.5 * (qc + sc[4] * delta[4]) + 0.5 * (slope * sign(sc[n]))
        lower.append(low_u)
        upper.append(high_u)
    half_dn = 0.5 * delta[n]
    lower += [half_dn + half_wa * delta[4], k_mean + k_flux, o_mean + o_flux]
    upper += [half_dn + half_wc * delta[4], k_mean - k_flux, o_mean - o_flux]
    lower += [rho_mean, heat, produced, slope]
    upper += [rho_mean, -heat, produced, slope]
    return lower, upper


def to_gradient(acc, cell):
    rho, u1, u2, u3, p, kt, om = cell["s"]
    inv_rho = 1.0 / rho
    inv_kt = 1.0 / kt
    half_wave = 0.5 * (acc[16] * cell["h"])
    heat = acc[14] * inv_rho
    y4 = acc[4]
    produced = ALPHA_OMEGA * (cell["m"][6] * acc[15]) * inv_kt
    d_rho = (
        acc[0]
        + acc[1] * u1
        + acc[2] * u2
        + acc[3] * u3
        + 0.5 * (y4 * (u1 * u1 + u2 * u2 + u3 * u3))
        + acc[5] * kt
        + acc[6] * om
        + acc[13]
        - (heat * p + half_wave) * inv_rho
    )
    return [
        d_rho,
        rho * (acc[1] + y4 * u1) + acc[7],
        rho * (acc[2] + y4 * u2) + acc[8],
        rho * (acc[3] + y4 * u3) + acc[9],
        y4 * (1.0 / (GAMMA - 1.0)) + acc[10] + heat + half_wave / p,
        rho * acc[5] + acc[11] - produced * (om * inv_kt),
        rho * acc[6] + acc[12] + produced,
    ]


def fluid_weight(code, adjoint):
    fluid = code != 1
    return [jnp.where(fluid, x, 0.0) for x in adjoint]


def pack_kernel(
    peers, links_in, farfield_in, flow_in, adj_in, codes_in, radial, pair, marks, far, links, farfield, states, weights, kinds, sems
):
    group, me = lax.axis_index("group"), lax.axis_index("block")
    copies = [pltpu.make_async_copy(links_in, links, sems.at[0]), pltpu.make_async_copy(farfield_in, farfield, sems.at[13])]
    for n, row in enumerate((0, 7)):
        copies.append(pltpu.make_async_copy(flow_in.at[:, :, row, :], states.at[n], sems.at[6 * n + 1]))
        copies.append(pltpu.make_async_copy(adj_in.at[:, :, row, :], weights.at[n], sems.at[6 * n + 2]))
        copies.append(pltpu.make_async_copy(codes_in.at[:, row, :], kinds.at[n], sems.at[6 * n + 3]))
        copies.append(pltpu.make_async_copy(flow_in.at[:, row], states.at[2 + n], sems.at[6 * n + 4]))
        copies.append(pltpu.make_async_copy(adj_in.at[:, row], weights.at[2 + n], sems.at[6 * n + 5]))
        copies.append(pltpu.make_async_copy(codes_in.at[row], kinds.at[2 + n], sems.at[6 * n + 6]))
    for copy in copies:
        copy.start()
    for copy in copies:
        copy.wait()

    upper_half = lax.broadcasted_iota(jnp.int32, (8, 128), 0) >= 4

    def layers(out, faces):
        goals = []
        for t, (n, partner) in enumerate(faces):
            fluid = kinds[n] != 1
            for v in range(NV):
                out[2 * NV * t + v] = states[n, v]
                out[2 * NV * t + NV + v] = jnp.where(fluid, weights[n, v], 0.0)
            goals.append(jnp.where(partner >= 0, lax.rem(partner, peers), -1).astype(jnp.float32))
        out[4 * NV] = jnp.where(upper_half, goals[1], goals[0])

    layers(radial, [(0, links[0, 2]), (1, links[0, 3])])
    even = lax.rem(group, 2) == 0
    forward, backward = (3, links[0, 1]), (2, links[0, 0])
    layers(
        pair,
        [
            [jnp.where(flag, x, y) for x, y in zip(forward, backward)]
            for flag in (even, jnp.logical_not(even))
        ],
    )
    for face in range(4):
        partner = links[0, face]
        if face < 2:
            source = jnp.where(even, 1 - face, face)
        else:
            source = lax.rem(jnp.maximum(partner, 0), peers) ^ me
        marks[face] = jnp.full((8, 128), jnp.where(partner >= 0, source, -1))
        marks[4 + face] = jnp.full((8, 128), links[1, face])
    for v in range(NV):
        far[v] = jnp.full((8, 128), farfield[v])


def relay_kernel(offsets, sources, outs_of, *refs):
    me = lax.axis_index("block")
    upper_half = lax.broadcasted_iota(jnp.int32, (8, 128), 0) >= 4
    kept = [[] for _ in offsets]
    for t, places in enumerate(sources):
        goals = [jnp.broadcast_to(refs[at][4 * NV, 4 * k : 4 * k + 1, :], (8, 128)) for at, k in places]
        for n, (offset, outs) in enumerate(zip(offsets, outs_of)):
            wanted = (me ^ offset).astype(jnp.float32)
            masks = [goal == wanted for goal in goals]
            found = functools.reduce(jnp.logical_or, masks)
            kept[n].append(jnp.where(found, wanted, -1.0))
            to, place = outs[t]
            for v in range(2 * NV):
                value, *others = [refs[at][2 * NV * k + v] for at, k in places]
                for x, mask in zip(others, masks[1:]):
                    value = jnp.where(mask, x, value)
                refs[to][2 * NV * place + v] = value
    for goals, outs in zip(kept, outs_of):
        if refs[outs[0][0]].shape[0] > 4 * NV:
            refs[outs[0][0]][4 * NV] = jnp.where(upper_half, goals[1], goals[0])


def interior_kernel(flow, adj, codes, out, carry):
    sublane = lax.broadcasted_iota(jnp.int32, (8, 128), 0)
    inside = sublane < 7

    def load(i):
        rows = pl.ds(pl.multiple_of(i * 8, 8), 8)
        raw = [adj[v, rows, :] for v in range(NV)]
        code = codes[rows, :]
        state = [flow[v, rows, :] for v in range(NV)]
        return prepare(state, fluid_weight(code, raw)), raw, code, rows

    carry[...] = jnp.zeros_like(carry)

    def step(i, _):
        cell, raw, code, rows = load(i)
        acc = [carry[n] for n in range(17)]
        for axis, dim, size, mask in ((2, 1, 128, None), (1, 0, 8, inside)):
            after = moved(cell, lambda x: pltpu.roll(x, size - 1, dim))
            lower, upper = face_pair(cell, after, axis, mask)
            acc = [t + lo + pltpu.roll(hi, 1, dim) for t, lo, hi in zip(acc, lower, upper)]

        def emit(acc):
            grad = to_gradient(acc, cell)
            rho, kt, om = cell["s"][0], cell["s"][5], cell["s"][6]
            w5, w6 = BETA_STAR * cell["m"][5], BETA_OMEGA * cell["m"][6]
            grad[0] -= (w5 * kt + w6 * om) * om
            grad[5] -= w5 * rho * om
            grad[6] -= (w5 * kt + 2.0 * w6 * om) * rho
            local = jnp.where(code == 2, DAMPING, jnp.where(code == 1, 1.0, 0.0))
            for v in range(NV):
                out[v, rows, :] = grad[v] + local * raw[v]

        @pl.when(i < 7)
        def _():
            lower, upper = face_pair(cell, load(i + 1)[0], 0)
            for n in range(17):
                carry[n] = upper[n]
            emit([t + lo for t, lo in zip(acc, lower)])

        @pl.when(i == 7)
        def _():
            emit(acc)

        return 0

    lax.fori_loop(0, 8, step, 0)


def rim_kernel(store, faces, plans, marks, far, grad, flow, adj, codes, *refs):
    if store:
        arrays, (out, ends, sems) = refs[:-3], refs[-3:]
        copies = []
        for n in range(2):
            rows = pl.ds(8 + 24 * n, 24)
            copies.append(pltpu.make_async_copy(grad.at[:, rows], out.at[:, rows], sems.at[2 + n]))
            copies[-1].start()
    else:
        arrays, out = refs[:-1], refs[-1]

    def ghosts(face):
        values = [far[v] for v in range(NV)] + [jnp.zeros((8, 128), jnp.float32)] * NV
        mark = marks[face]
        for at, t, steps in plans[face]:
            mask = functools.reduce(jnp.logical_or, [mark == step for step in steps])
            values = [jnp.where(mask, arrays[at][2 * NV * t + v], value) for v, value in enumerate(values)]
        return values

    lane = lax.broadcasted_iota(jnp.int32, (8, 128), 1)
    spans = (pl.ds(0, 8), pl.ds(56, 8), pl.ds(0, 8, stride=8), pl.ds(7, 8, stride=8))
    shares = []
    for face in faces:
        rows = spans[face]
        turned = marks[4 + face] == 1
        index = jnp.where(turned, 127 - lane, lane)
        values = [jnp.take_along_axis(x, index, axis=1) for x in ghosts(face)]
        swirl = jnp.where(turned, -1.0, 1.0)
        for v in (3, NV + 3):
            values[v] = values[v] * swirl
        other = prepare(values[:NV], values[NV:])
        state = [flow[v, rows, :] for v in range(NV)]
        weight = fluid_weight(codes[rows, :], [adj[v, rows, :] for v in range(NV)])
        cell = prepare(state, weight)
        if face % 2 == 0:
            acc = face_pair(other, cell, face // 2)[1]
        else:
            acc = face_pair(cell, other, face // 2)[0]
        shares.append(to_gradient(acc, cell))
    if store:
        for n, share in enumerate(shares):
            for v in range(NV):
                ends[n, v] = grad[v, spans[faces[n]], :] + share[v]
            copies.append(pltpu.make_async_copy(ends.at[n], out.at[:, pl.ds(56 * n, 8)], sems.at[n]))
            copies[-1].start()
        for copy in copies:
            copy.wait()
        return
    out[...] = grad[...]
    for v in range(NV):
        for rows, share in zip([spans[f] for f in faces], shares):
            out[v, rows, :] = out[v, rows, :] + share[v]

def shape(*dims, dtype=jnp.float32):
    return jax.ShapeDtypeStruct(dims, dtype)


def span(basis):
    offsets = [0]
    for b in basis:
        offsets += [o ^ b for o in offsets]
    return offsets


def solution(mesh):
    groups, peers = mesh.shape["group"], mesh.shape["block"]
    bits = peers.bit_length() - 1
    basis = [1 << i for i in range(bits - 1)] + [peers // 2]

    def within(offset):
        return [
            (g * peers + h, g * peers + (h ^ offset)) for g in range(groups) for h in range(peers)
        ]

    def between(first, offset):
        pairs = []
        for g in range(groups):
            other = (g + 1 if (g % 2 == 0) == first else g - 1) % groups
            pairs += [(g * peers + h, other * peers + (h ^ offset)) for h in range(peers)]
        return pairs

    def relay(offsets, sources, rows=4 * NV, split=False):
        arrays = []
        for x, _ in sum(sources, []):
            if not any(x is y for y in arrays):
                arrays.append(x)
        places = [[(next(n for n, y in enumerate(arrays) if y is x), k) for x, k in held] for held in sources]
        kinds, base = len(sources), len(arrays)
        if split:
            outs_of = [[(base + n * kinds + t, 0) for t in range(kinds)] for n in range(len(offsets))]
            outs = [shape(2 * NV, 8, 128)] * (len(offsets) * kinds)
        else:
            outs_of = [[(base + n, t) for t in range(kinds)] for n in range(len(offsets))]
            outs = [shape(rows, 8, 128)] * len(offsets)
        return pl.pallas_call(
            functools.partial(relay_kernel, offsets, places, outs_of),
            out_shape=outs,
            in_specs=[VMEM] * base,
            out_specs=[VMEM] * len(outs),
            compiler_params=PARAMS,
            name="relay",
        )(*arrays)

    def spread(bundle, steps):
        held = {0: bundle}
        for b in steps:
            for o in list(held):
                held[o ^ b] = lax.ppermute(held[o], AXES, within(b))
        return held

    def per_device(flow_state, adjoint, cell_codes, block_links, farfield):
        links = jnp.transpose(block_links[0])
        flow, adj, codes = flow_state.reshape(NV, 64, 128), adjoint.reshape(NV, 64, 128), cell_codes.reshape(64, 128)
        hbm = [pltpu.with_memory_space_constraint(x, pltpu.HBM) for x in (links, farfield, flow_state[0], adjoint[0], cell_codes[0])]
        radial, pair, marks, outer = pl.pallas_call(
            functools.partial(pack_kernel, peers),
            out_shape=[shape(4 * NV + 1, 8, 128)] * 2 + [shape(8, 8, 128, dtype=jnp.int32), shape(NV, 8, 128)],
            in_specs=[pl.BlockSpec(memory_space=pltpu.HBM)] * 5,
            out_specs=[VMEM] * 4,
            scratch_shapes=[
                pltpu.SMEM((2, 4), jnp.int32),
                pltpu.SMEM((NV,), jnp.float32),
                pltpu.VMEM((4, NV, 8, 128), jnp.float32),
                pltpu.VMEM((4, NV, 8, 128), jnp.float32),
                pltpu.VMEM((4, 8, 128), jnp.int32),
                pltpu.SemaphoreType.DMA((14,)),
            ],
            compiler_params=PARAMS,
            name="pack",
        )(*hbm)
        held_r = spread(radial, basis[:-1][::-1])
        held_a = spread(pair, basis[-1:])
        near = sorted(span(basis[:-1])[1:], key=lambda o: (not o & 1, o))
        onward = relay(near, [[(x, t) for x in held_a.values()] for t in range(2)], rows=4 * NV + 1)
        last = list(held_a.values()) + [lax.ppermute(x, AXES, within(o)) for o, x in zip(near, onward)]
        inner = pl.pallas_call(
            interior_kernel,
            out_shape=shape(NV, 64, 128),
            in_specs=[VMEM] * 3,
            out_specs=VMEM,
            scratch_shapes=[pltpu.VMEM((17, 8, 128), jnp.float32)],
            compiler_params=PARAMS,
            cost_estimate=pl.CostEstimate(flops=6000000, bytes_accessed=800000, transcendentals=60000),
            name="interior",
        )(flow, adj, codes)
        first = len(held_a)
        inner, last[first] = lax.optimization_barrier((inner, last[first]))
        choices = [[(x, t) for x in last] for t in range(2)]
        even_pair, odd_pair = relay([0], choices, split=True)
        even_pair = lax.ppermute(even_pair, AXES, between(True, 0))
        odd_pair = lax.ppermute(odd_pair, AXES, between(False, 0))
        far = span(basis[-1:])[1:]
        onward = relay(far, [[(x, t) for x in held_r.values()] for t in range(2)])
        sent = {o: lax.ppermute(x, AXES, within(o)) for o, x in zip(far, onward)}
        axial_plan = [(0, 0, [0]), (1, 0, [1])]
        plan = [(x, [n]) for n, x in held_r.items() if n]
        plan += [(x, [n ^ o for n in held_r]) for o, x in sent.items()]
        low, high = [[(n, t, steps) for n, (_, steps) in enumerate(plan)] for t in range(2)]
        plans = [axial_plan, axial_plan, high, low]
        result = inner
        for faces, arrays in (((2, 3), [x for x, _ in plan]), ((0, 1), [even_pair, odd_pair])):
            store = faces[0] == 0
            result = pl.pallas_call(
                functools.partial(rim_kernel, store, faces, plans),
                out_shape=shape(NV, 64, 128),
                in_specs=[VMEM] * (6 + len(arrays)),
                out_specs=pl.BlockSpec(memory_space=pltpu.HBM) if store else VMEM,
                scratch_shapes=[pltpu.VMEM((2, NV, 8, 128), jnp.float32), pltpu.SemaphoreType.DMA((4,))] if store else [],
                compiler_params=PARAMS,
                cost_estimate=pl.CostEstimate(flops=1000000, bytes_accessed=900000, transcendentals=20000),
                name="rim",
            )(marks, outer, result, flow, adj, codes, *arrays)
        return result.reshape(flow_state.shape)

    spec = P(("group", "block"), None, None, None, None)
    return jax.shard_map(
        per_device,
        mesh=mesh,
        in_specs=(
            spec,
            spec,
            P(("group", "block"), None, None, None),
            P(("group", "block"), None, None),
            P(),
        ),
        out_specs=spec,
        check_vma=False,
    )
```

```python
import functools

import jax
import jax.numpy as jnp
from jax import lax
from jax.experimental import pallas as pl
from jax.experimental.pallas import tpu as pltpu
from jax.sharding import PartitionSpec as P

GAMMA = 1.4
MU_LAMINAR = 0.02
KAPPA_HEAT = 0.07
SIGMA_K = 0.85
SIGMA_OMEGA = 0.5
BETA_STAR = 0.09
BETA_OMEGA = 0.075
ALPHA_OMEGA = 0.52
INV_A1_SQ = 1.0 / (0.31 * 0.31)
DAMPING = 2.0

NV = 7
AXES = ("group", "block")
VMEM = pl.BlockSpec(memory_space=pltpu.VMEM)
SMEM = pl.BlockSpec(memory_space=pltpu.SMEM)
PARAMS = pltpu.CompilerParams(vmem_limit_bytes=24 << 20)


def prepare(state, weight):
    rho, u1, u2, u3, p, kt, om = state
    half_rho = 0.5 * rho
    cons = [
        rho,
        rho * u1,
        rho * u2,
        rho * u3,
        p * (1.0 / (GAMMA - 1.0)) + half_rho * (u1 * u1 + u2 * u2 + u3 * u3),
        rho * kt,
        rho * om,
    ]
    half_sound = 0.5 * jnp.sqrt(GAMMA * (p / rho))
    produce = weight[5] + (ALPHA_OMEGA * weight[6]) * (om / kt)
    return dict(s=state, m=weight, q=cons, h=half_sound, v=produce)


def moved(cell, shift):
    return dict(
        s=[shift(x) for x in cell["s"]],
        m=[shift(x) for x in cell["m"]],
        q=[shift(x) for x in cell["q"]],
        h=shift(cell["h"]),
        v=shift(cell["v"]),
    )


def sign(x):
    return jnp.where(x > 0.0, 1.0, jnp.where(x < 0.0, -1.0, 0.0))


def face_pair(low, high, axis, mask=None):
    n = 1 + axis
    sa, sc = low["s"], high["s"]
    delta = [c - a for a, c in zip(low["m"], high["m"])]
    weight_sum = low["v"] + high["v"]
    if mask is not None:
        delta = [jnp.where(mask, d, 0.0) for d in delta]
        weight_sum = jnp.where(mask, weight_sum, 0.0)
    qa = functools.reduce(jnp.add, [d * q for d, q in zip(delta, low["q"])])
    qc = functools.reduce(jnp.add, [d * q for d, q in zip(delta, high["q"])])
    half_wa, half_wc = 0.5 * sa[n], 0.5 * sc[n]
    half_lam = 0.5 * (jnp.abs(half_wa) + jnp.abs(half_wc) + low["h"] + high["h"])
    ca, cc = half_wa + half_lam, half_wc - half_lam
    slope = 0.5 * (qa - qc)

    e = [sc[i] - sa[i] for i in (1, 2, 3)]
    half_d4 = 0.5 * delta[4]
    g = [delta[i] + half_d4 * (sa[i] + sc[i]) for i in (1, 2, 3)]
    strain = e[0] * e[0] + e[1] * e[1] + e[2] * e[2]
    eg = e[0] * g[0] + e[1] * g[1] + e[2] * g[2]
    rho_m = 0.5 * (sa[0] + sc[0])
    kt_m = 0.5 * (sa[5] + sc[5])
    om_m = 0.5 * (sa[6] + sc[6])
    inv = lax.rsqrt(om_m * om_m + strain * INV_A1_SQ)
    mut = rho_m * kt_m * inv
    d_mut = (
        0.5 * (strain * weight_sum)
        - eg
        - SIGMA_K * (delta[5] * (sc[5] - sa[5]))
        - SIGMA_OMEGA * (delta[6] * (sc[6] - sa[6]))
    )
    nu = MU_LAMINAR + mut
    limited = d_mut * mut * (inv * inv)
    along = mut * weight_sum - limited * INV_A1_SQ
    k_flux = delta[5] * (MU_LAMINAR + SIGMA_K * mut)
    o_flux = delta[6] * (MU_LAMINAR + SIGMA_OMEGA * mut)
    half_inv = 0.5 * (d_mut * inv)
    k_mean = half_inv * rho_m
    rho_mean = half_inv * kt_m
    o_mean = -0.5 * (limited * om_m)
    heat = KAPPA_HEAT * delta[4]
    produced = 0.5 * (mut * strain)
    if mask is not None:
        produced = jnp.where(mask, produced, 0.0)
    side = nu * half_d4
    lower = [ca * d for d in delta]
    upper = [cc * d for d in delta]
    for i in range(3):
        jump = along * e[i] - nu * g[i]
        mean = side * e[i]
        low_u, high_u = -jump - mean, jump - mean
        if i == axis:
            low_u += 0.5 * (qa + sa[4] * delta[4]) + 0.5 * (slope * sign(sa[n]))
            high_u += 0.5 * (qc + sc[4] * delta[4]) + 0.5 * (slope * sign(sc[n]))
        lower.append(low_u)
        upper.append(high_u)
    half_dn = 0.5 * delta[n]
    lower += [half_dn + half_wa * delta[4], k_mean + k_flux, o_mean + o_flux]
    upper += [half_dn + half_wc * delta[4], k_mean - k_flux, o_mean - o_flux]
    lower += [rho_mean, heat, produced, slope]
    upper += [rho_mean, -heat, produced, slope]
    return lower, upper


def to_gradient(acc, cell):
    rho, u1, u2, u3, p, kt, om = cell["s"]
    inv_rho = 1.0 / rho
    inv_kt = 1.0 / kt
    half_wave = 0.5 * (acc[16] * cell["h"])
    heat = acc[14] * inv_rho
    y4 = acc[4]
    produced = ALPHA_OMEGA * (cell["m"][6] * acc[15]) * inv_kt
    d_rho = (
        acc[0]
        + acc[1] * u1
        + acc[2] * u2
        + acc[3] * u3
        + 0.5 * (y4 * (u1 * u1 + u2 * u2 + u3 * u3))
        + acc[5] * kt
        + acc[6] * om
        + acc[13]
        - (heat * p + half_wave) * inv_rho
    )
    return [
        d_rho,
        rho * (acc[1] + y4 * u1) + acc[7],
        rho * (acc[2] + y4 * u2) + acc[8],
        rho * (acc[3] + y4 * u3) + acc[9],
        y4 * (1.0 / (GAMMA - 1.0)) + acc[10] + heat + half_wave / p,
        rho * acc[5] + acc[11] - produced * (om * inv_kt),
        rho * acc[6] + acc[12] + produced,
    ]


def fluid_weight(code, adjoint):
    fluid = code != 1
    return [jnp.where(fluid, x, 0.0) for x in adjoint]


def pack_kernel(
    peers, links_in, farfield_in, flow_in, adj_in, codes_in, radial, pair, marks, far, links, farfield, states, weights, kinds, sems
):
    group, me = lax.axis_index("group"), lax.axis_index("block")
    copies = [pltpu.make_async_copy(links_in, links, sems.at[0]), pltpu.make_async_copy(farfield_in, farfield, sems.at[13])]
    for n, row in enumerate((0, 7)):
        copies.append(pltpu.make_async_copy(flow_in.at[:, :, row, :], states.at[n], sems.at[6 * n + 1]))
        copies.append(pltpu.make_async_copy(adj_in.at[:, :, row, :], weights.at[n], sems.at[6 * n + 2]))
        copies.append(pltpu.make_async_copy(codes_in.at[:, row, :], kinds.at[n], sems.at[6 * n + 3]))
        copies.append(pltpu.make_async_copy(flow_in.at[:, row], states.at[2 + n], sems.at[6 * n + 4]))
        copies.append(pltpu.make_async_copy(adj_in.at[:, row], weights.at[2 + n], sems.at[6 * n + 5]))
        copies.append(pltpu.make_async_copy(codes_in.at[row], kinds.at[2 + n], sems.at[6 * n + 6]))
    for copy in copies:
        copy.start()
    for copy in copies:
        copy.wait()

    upper_half = lax.broadcasted_iota(jnp.int32, (8, 128), 0) >= 4

    def layers(out, faces):
        goals = []
        for t, (n, partner) in enumerate(faces):
            fluid = kinds[n] != 1
            for v in range(NV):
                out[2 * NV * t + v] = states[n, v]
                out[2 * NV * t + NV + v] = jnp.where(fluid, weights[n, v], 0.0)
            goals.append(jnp.where(partner >= 0, lax.rem(partner, peers), -1).astype(jnp.float32))
        out[4 * NV] = jnp.where(upper_half, goals[1], goals[0])

    layers(radial, [(0, links[0, 2]), (1, links[0, 3])])
    even = lax.rem(group, 2) == 0
    forward, backward = (3, links[0, 1]), (2, links[0, 0])
    layers(
        pair,
        [
            [jnp.where(flag, x, y) for x, y in zip(forward, backward)]
            for flag in (even, jnp.logical_not(even))
        ],
    )
    for face in range(4):
        partner = links[0, face]
        if face < 2:
            source = jnp.where(even, 1 - face, face)
        else:
            source = lax.rem(jnp.maximum(partner, 0), peers) ^ me
        marks[face] = jnp.full((8, 128), jnp.where(partner >= 0, source, -1))
        marks[4 + face] = jnp.full((8, 128), links[1, face])
    for v in range(NV):
        far[v] = jnp.full((8, 128), farfield[v])


def relay_kernel(offsets, sources, outs_of, *refs):
    me = lax.axis_index("block")
    upper_half = lax.broadcasted_iota(jnp.int32, (8, 128), 0) >= 4
    kept = [[] for _ in offsets]
    for t, places in enumerate(sources):
        goals = [jnp.broadcast_to(refs[at][4 * NV, 4 * k : 4 * k + 1, :], (8, 128)) for at, k in places]
        for n, (offset, outs) in enumerate(zip(offsets, outs_of)):
            wanted = (me ^ offset).astype(jnp.float32)
            masks = [goal == wanted for goal in goals]
            found = functools.reduce(jnp.logical_or, masks)
            kept[n].append(jnp.where(found, wanted, -1.0))
            to, place = outs[t]
            for v in range(2 * NV):
                value, *others = [refs[at][2 * NV * k + v] for at, k in places]
                for x, mask in zip(others, masks[1:]):
                    value = jnp.where(mask, x, value)
                refs[to][2 * NV * place + v] = value
    for goals, outs in zip(kept, outs_of):
        if refs[outs[0][0]].shape[0] > 4 * NV:
            refs[outs[0][0]][4 * NV] = jnp.where(upper_half, goals[1], goals[0])


def interior_kernel(flow, adj, codes, out, carry):
    sublane = lax.broadcasted_iota(jnp.int32, (8, 128), 0)
    inside = sublane < 7

    def load(i):
        rows = pl.ds(pl.multiple_of(i * 8, 8), 8)
        raw = [adj[v, rows, :] for v in range(NV)]
        code = codes[rows, :]
        state = [flow[v, rows, :] for v in range(NV)]
        return prepare(state, fluid_weight(code, raw)), raw, code, rows

    carry[...] = jnp.zeros_like(carry)

    def step(i, _):
        cell, raw, code, rows = load(i)
        acc = [carry[n] for n in range(17)]
        for axis, dim, size, mask in ((2, 1, 128, None), (1, 0, 8, inside)):
            after = moved(cell, lambda x: pltpu.roll(x, size - 1, dim))
            lower, upper = face_pair(cell, after, axis, mask)
            acc = [t + lo + pltpu.roll(hi, 1, dim) for t, lo, hi in zip(acc, lower, upper)]

        def emit(acc):
            grad = to_gradient(acc, cell)
            rho, kt, om = cell["s"][0], cell["s"][5], cell["s"][6]
            w5, w6 = BETA_STAR * cell["m"][5], BETA_OMEGA * cell["m"][6]
            grad[0] -= (w5 * kt + w6 * om) * om
            grad[5] -= w5 * rho * om
            grad[6] -= (w5 * kt + 2.0 * w6 * om) * rho
            local = jnp.where(code == 2, DAMPING, jnp.where(code == 1, 1.0, 0.0))
            for v in range(NV):
                out[v, rows, :] = grad[v] + local * raw[v]

        @pl.when(i < 7)
        def _():
            lower, upper = face_pair(cell, load(i + 1)[0], 0)
            for n in range(17):
                carry[n] = upper[n]
            emit([t + lo for t, lo in zip(acc, lower)])

        @pl.when(i == 7)
        def _():
            emit(acc)

        return 0

    lax.fori_loop(0, 8, step, 0)


def rim_kernel(faces, plans, marks, far, grad, flow, adj, codes, *refs):
    arrays, out = refs[:-1], refs[-1]

    def ghosts(face):
        values = [far[v] for v in range(NV)] + [jnp.zeros((8, 128), jnp.float32)] * NV
        mark = marks[face]
        for at, t, steps in plans[face]:
            mask = functools.reduce(jnp.logical_or, [mark == step for step in steps])
            values = [jnp.where(mask, arrays[at][2 * NV * t + v], value) for v, value in enumerate(values)]
        return values

    lane = lax.broadcasted_iota(jnp.int32, (8, 128), 1)
    spans = (pl.ds(0, 8), pl.ds(56, 8), pl.ds(0, 8, stride=8), pl.ds(7, 8, stride=8))
    shares = []
    for face in faces:
        rows = spans[face]
        turned = marks[4 + face] == 1
        index = jnp.where(turned, 127 - lane, lane)
        values = [jnp.take_along_axis(x, index, axis=1) for x in ghosts(face)]
        swirl = jnp.where(turned, -1.0, 1.0)
        for v in (3, NV + 3):
            values[v] = values[v] * swirl
        other = prepare(values[:NV], values[NV:])
        state = [flow[v, rows, :] for v in range(NV)]
        weight = fluid_weight(codes[rows, :], [adj[v, rows, :] for v in range(NV)])
        cell = prepare(state, weight)
        if face % 2 == 0:
            acc = face_pair(other, cell, face // 2)[1]
        else:
            acc = face_pair(cell, other, face // 2)[0]
        shares.append(to_gradient(acc, cell))
    out[...] = grad[...]
    for v in range(NV):
        for rows, share in zip([spans[f] for f in faces], shares):
            out[v, rows, :] = out[v, rows, :] + share[v]

def shape(*dims, dtype=jnp.float32):
    return jax.ShapeDtypeStruct(dims, dtype)


def span(basis):
    offsets = [0]
    for b in basis:
        offsets += [o ^ b for o in offsets]
    return offsets


def solution(mesh):
    groups, peers = mesh.shape["group"], mesh.shape["block"]
    bits = peers.bit_length() - 1
    basis = [1 << i for i in range(bits - 1)] + [peers // 2]

    def within(offset):
        return [
            (g * peers + h, g * peers + (h ^ offset)) for g in range(groups) for h in range(peers)
        ]

    def between(first, offset):
        pairs = []
        for g in range(groups):
            other = (g + 1 if (g % 2 == 0) == first else g - 1) % groups
            pairs += [(g * peers + h, other * peers + (h ^ offset)) for h in range(peers)]
        return pairs

    def relay(offsets, sources, rows=4 * NV, split=False):
        arrays = []
        for x, _ in sum(sources, []):
            if not any(x is y for y in arrays):
                arrays.append(x)
        places = [[(next(n for n, y in enumerate(arrays) if y is x), k) for x, k in held] for held in sources]
        kinds, base = len(sources), len(arrays)
        if split:
            outs_of = [[(base + n * kinds + t, 0) for t in range(kinds)] for n in range(len(offsets))]
            outs = [shape(2 * NV, 8, 128)] * (len(offsets) * kinds)
        else:
            outs_of = [[(base + n, t) for t in range(kinds)] for n in range(len(offsets))]
            outs = [shape(rows, 8, 128)] * len(offsets)
        return pl.pallas_call(
            functools.partial(relay_kernel, offsets, places, outs_of),
            out_shape=outs,
            in_specs=[VMEM] * base,
            out_specs=[VMEM] * len(outs),
            compiler_params=PARAMS,
            name="relay",
        )(*arrays)

    def spread(bundle, steps):
        held = {0: bundle}
        for b in steps:
            for o in list(held):
                held[o ^ b] = lax.ppermute(held[o], AXES, within(b))
        return held

    def per_device(flow_state, adjoint, cell_codes, block_links, farfield):
        links = jnp.transpose(block_links[0])
        flow, adj, codes = flow_state.reshape(NV, 64, 128), adjoint.reshape(NV, 64, 128), cell_codes.reshape(64, 128)
        hbm = [pltpu.with_memory_space_constraint(x, pltpu.HBM) for x in (links, farfield, flow_state[0], adjoint[0], cell_codes[0])]
        radial, pair, marks, outer = pl.pallas_call(
            functools.partial(pack_kernel, peers),
            out_shape=[shape(4 * NV + 1, 8, 128)] * 2 + [shape(8, 8, 128, dtype=jnp.int32), shape(NV, 8, 128)],
            in_specs=[pl.BlockSpec(memory_space=pltpu.HBM)] * 5,
            out_specs=[VMEM] * 4,
            scratch_shapes=[
                pltpu.SMEM((2, 4), jnp.int32),
                pltpu.SMEM((NV,), jnp.float32),
                pltpu.VMEM((4, NV, 8, 128), jnp.float32),
                pltpu.VMEM((4, NV, 8, 128), jnp.float32),
                pltpu.VMEM((4, 8, 128), jnp.int32),
                pltpu.SemaphoreType.DMA((14,)),
            ],
            compiler_params=PARAMS,
            name="pack",
        )(*hbm)
        held_r = spread(radial, basis[:-1][::-1])
        held_a = spread(pair, basis[-1:])
        near = sorted(span(basis[:-1])[1:], key=lambda o: (not o & 1, o))
        onward = relay(near, [[(x, t) for x in held_a.values()] for t in range(2)], rows=4 * NV + 1)
        last = list(held_a.values()) + [lax.ppermute(x, AXES, within(o)) for o, x in zip(near, onward)]
        inner = pl.pallas_call(
            interior_kernel,
            out_shape=shape(NV, 64, 128),
            in_specs=[VMEM] * 3,
            out_specs=VMEM,
            scratch_shapes=[pltpu.VMEM((17, 8, 128), jnp.float32)],
            compiler_params=PARAMS,
            cost_estimate=pl.CostEstimate(flops=6000000, bytes_accessed=800000, transcendentals=60000),
            name="interior",
        )(flow, adj, codes)
        first = len(held_a)
        inner, last[first] = lax.optimization_barrier((inner, last[first]))
        choices = [[(x, t) for x in last] for t in range(2)]
        even_pair, odd_pair = relay([0], choices, split=True)
        odd_pair = lax.ppermute(odd_pair, AXES, between(False, 0))
        even_pair = lax.ppermute(even_pair, AXES, between(True, 0))
        far = span(basis[-1:])[1:]
        onward = relay(far, [[(x, t) for x in held_r.values()] for t in range(2)])
        sent = {o: lax.ppermute(x, AXES, within(o)) for o, x in zip(far, onward)}
        axial_plan = [(0, 0, [0]), (1, 0, [1])]
        plan = [(x, [n]) for n, x in held_r.items() if n]
        plan += [(x, [n ^ o for n in held_r]) for o, x in sent.items()]
        low, high = [[(n, t, steps) for n, (_, steps) in enumerate(plan)] for t in range(2)]
        plans = [axial_plan, axial_plan, high, low]
        result = inner
        for faces, arrays in (((2, 3), [x for x, _ in plan]), ((0, 1), [even_pair, odd_pair])):
            result = pl.pallas_call(
                functools.partial(rim_kernel, faces, plans),
                out_shape=shape(NV, 64, 128),
                in_specs=[VMEM] * (6 + len(arrays)),
                out_specs=VMEM,
                compiler_params=PARAMS,
                cost_estimate=pl.CostEstimate(flops=1000000, bytes_accessed=900000, transcendentals=20000),
                name="rim",
            )(marks, outer, result, flow, adj, codes, *arrays)
        return result.reshape(flow_state.shape)

    spec = P(("group", "block"), None, None, None, None)
    return jax.shard_map(
        per_device,
        mesh=mesh,
        in_specs=(
            spec,
            spec,
            P(("group", "block"), None, None, None),
            P(("group", "block"), None, None),
            P(),
        ),
        out_specs=spec,
        check_vma=False,
    )
```
